32 devices in a mesh: rows: 16 (over z, x, core), split: 2 (over y).
Axes of the slice: x: 2, y: 2, z: 4, core: 2. Of those that a mesh axis runs over, the one named last changes fastest.
Arguments:
- embeddings: bfloat16 [8192, 768], P(('rows', 'split')), may hold values from -24 to 24
- cluster_id: int32 [8192], P(('rows', 'split')), may hold values from 0 to 127, as said below
- owner_map: int32 [128], replicated, may hold values from 0 to 15, as said below
Outputs:
- prune_score: float32 [8192], P(('rows', 'split'))
The draws below stay inside these ranges and needn't reach their ends.
Inputs may be any that keep to these rules, and one draw needn't show every extreme that they name: `owner_map`: every group 0 to 15 holds exactly 8 clusters. `cluster_id`: within each aligned block of 256 rows (the rows of one device), no group holds more than 32 of the block's rows, and one group holds exactly 32; every group holds exactly 32 rows of some block. Every cluster holds two rows or more.
All inputs are finite; a program needn't handle non-finite values.
Results may differ from the reference program's by a relative error of at most 0.0005.
Values may be sent and summed in bfloat16 or wider, within the bound.
A program may use at most 64 MiB of HBM per device.

```python
import math
import jax
import jax.numpy as jnp
from jax import lax

D = 768
ROW_DEV = 256
CL_DEV = 8
CAP = 32
CLUSTERS = 128
ROWS = 8192


def group_permutation(key):
    return jax.random.permutation(jax.random.fold_in(key, 11), CLUSTERS)


def cluster_layout(key):
    owners = CLUSTERS // CL_DEV
    blocks = ROWS // ROW_DEV
    inverse = jnp.argsort(group_permutation(key))
    offset = jax.random.randint(jax.random.fold_in(key, 12), (), 0, owners)
    block_range = jnp.arange(blocks)
    full_owner = (block_range + offset) % owners
    pair_shift = block_range // owners * (CAP // 2)
    block_keys = jax.random.split(jax.random.fold_in(key, 13), blocks)

    def one_block(block_key, chosen, shift):
        first_key, second_key, third_key = jax.random.split(block_key, 3)
        others = jax.random.permutation(first_key, (owners - 1) * CAP)[:ROW_DEV - CAP] // CAP
        others = others + (others >= chosen).astype(others.dtype)
        listed = jnp.concatenate([jnp.full((CAP,), chosen, others.dtype), others])
        paired = ((jnp.arange(CAP) // 2 + shift) % CL_DEV).astype(jnp.int32)
        loose = jax.random.randint(third_key, (ROW_DEV - CAP,), 0, CL_DEV).astype(jnp.int32)
        member = jnp.concatenate([paired, loose])
        order = jax.random.permutation(second_key, ROW_DEV)
        return inverse[listed[order] * CL_DEV + member[order]]
    return jax.vmap(one_block)(block_keys, full_owner, pair_shift).reshape(-1).astype(jnp.int32)


def draw_owner_map(key, part):
    return (group_permutation(key) // CL_DEV).astype(jnp.int32)


def draw_cluster_id(key, part):
    return cluster_layout(key)


def draw_embeddings(key, part):
    clusters = cluster_layout(key)
    centre_key = jax.random.fold_in(key, 21)
    spread_key = jax.random.fold_in(key, 22)
    noise_key = jax.random.fold_in(key, 23)
    centres = 0.35 * jnp.clip(jax.random.normal(centre_key, (CLUSTERS, D), jnp.float32), -6.0, 6.0)
    spread = jnp.exp(jax.random.uniform(spread_key, (ROWS, 1), jnp.float32, math.log(0.5), math.log(2.0)))
    noise_rows = jnp.clip(jax.random.normal(noise_key, (ROWS, D), jnp.float32), -6.0, 6.0)
    return (centres[clusters] + spread * noise_rows).astype(jnp.bfloat16)


def setup_inputs(seed: int = 0) -> dict:
    seeds = jax.random.split(jax.random.key(seed), 4)
    return {
        "embeddings": draw_embeddings(jax.random.fold_in(seeds[3], 71), 0),
        "cluster_id": draw_cluster_id(jax.random.fold_in(seeds[3], 71), 0),
        "owner_map": draw_owner_map(jax.random.fold_in(seeds[3], 71), 0),
    }


FLOOR_SCORE = -1e+30

def reference(embeddings, cluster_id, owner_map):
    owners = CLUSTERS // CL_DEV
    blocks = ROWS // ROW_DEV
    owner_of = owner_map[cluster_id]
    by_block = owner_of.reshape(blocks, ROW_DEV)
    earlier = jnp.arange(ROW_DEV)[None, :] < jnp.arange(ROW_DEV)[:, None]
    ranking = lax.optimization_barrier(jnp.sum((by_block[:, :, None] == by_block[:, None, :]) & earlier[None], axis=2))
    placing = (jnp.arange(blocks, dtype=jnp.int32)[:, None] * CAP + ranking.astype(jnp.int32)).reshape(-1)
    member_table = jnp.full((owners, blocks * CAP), -1, jnp.int32).at[owner_of, placing].set(jnp.arange(ROWS, dtype=jnp.int32))
    score_scale = 1.0 / math.sqrt(D)

    def one_group(members):
        present = members >= 0
        clipped = jnp.maximum(members, 0)
        member_rows = embeddings[clipped]
        member_ids = jnp.where(present, cluster_id[clipped], -1)
        scores = jnp.dot(member_rows, member_rows.T, preferred_element_type=jnp.float32) * score_scale
        group_size = members.shape[0]
        same_cluster = member_ids[:, None] == member_ids[None, :]
        allowed = present[None, :] & same_cluster & (jnp.arange(group_size)[:, None] != jnp.arange(group_size)[None, :])
        masked = jnp.where(allowed, scores, FLOOR_SCORE)
        highest = lax.optimization_barrier(jnp.max(masked, axis=1))
        totals = lax.optimization_barrier(jnp.sum(jnp.where(allowed, jnp.exp(masked - highest[:, None]), 0.0), axis=1))
        return highest + jnp.log(totals)
    density = lax.map(one_group, member_table)
    flat_members = member_table.reshape(-1)
    flat_density = density.reshape(-1)
    present = flat_members >= 0
    member_cluster = jnp.where(present, cluster_id[jnp.maximum(flat_members, 0)], CLUSTERS)
    sum_density = jax.ops.segment_sum(jnp.where(present, flat_density, 0.0), member_cluster, CLUSTERS + 1)[:CLUSTERS]
    counts = jax.ops.segment_sum(present.astype(jnp.float32), member_cluster, CLUSTERS + 1)[:CLUSTERS]
    cluster_mean = sum_density / jnp.maximum(counts, 1.0)
    scores_out = jnp.where(present, flat_density - cluster_mean[jnp.minimum(member_cluster, CLUSTERS - 1)], 0.0)
    target = jnp.where(present, flat_members, ROWS)
    return jnp.zeros((ROWS + 1,), jnp.float32).at[target].set(scores_out)[:ROWS]
```

```python
import functools

import jax
import jax.numpy as jnp
from jax import lax
from jax.experimental import pallas as pl
from jax.experimental.pallas import tpu as pltpu
from jax.sharding import PartitionSpec as P

FLOOR_SCORE = -1e30
LANES = 128
KEY_CHUNK = 256
MESH = pl.DeviceIdType.MESH
F32 = jnp.float32
BF16 = jnp.bfloat16


def iota(shape, dim):
    return lax.broadcasted_iota(jnp.int32, shape, dim)


def one_hot(hit, dtype=BF16):
    return jnp.where(hit, 1.0, 0.0).astype(dtype)


def dot(a, b, dims=((1,), (0,)), precision=None):
    return lax.dot_general(a, b, (dims, ((), ())), preferred_element_type=F32, precision=precision)


def column_to_row(column):
    blocks = [
        jnp.transpose(jnp.broadcast_to(column[at : at + LANES], (LANES, LANES)))[0:1]
        for at in range(0, column.shape[0], LANES)
    ]
    return jnp.concatenate(blocks, axis=1)


def kernel(
    groups, parts, local_clusters,
    emb_in, cid_in, owner_in, out_ref,
    emb_ref, cid_ref, owner_ref,
    outgoing, out_ids, keys, key_ids, id_rows, id_cols, scores, result, returned,
    send_sem, recv_sem, id_send, id_recv, fwd_send, fwd_recv, idf_send, idf_recv,
    ret_send, ret_recv, local_sem, load_sem,
):
    rows_here, width = emb_ref.shape
    clusters_all = owner_ref.shape[1]
    cap = outgoing.shape[1]
    per_row = LANES // cap
    slots = groups * cap
    lane_rows = slots // LANES
    r, s = lax.axis_index("rows"), lax.axis_index("split")
    me = (r // parts) * parts + s
    part = r % parts

    def device(group, piece):
        return ((group // parts) * parts + piece, group % parts)

    def step_offset(t):
        half = (t + 1) // 2
        return groups // 2 + half - 2 * half * ((t + 1) % 2)

    def peer_out(t):
        return (me + step_offset(t)) % groups

    def peer_in(t):
        return (me + groups - step_offset(t)) % groups

    def sibling(d):
        return (part + d) % parts

    barrier = pltpu.get_barrier_semaphore()

    def each(first, action):
        @pl.loop(first, groups, unroll=groups <= 16)
        def _(k):
            inner = ((me // 4) == 1) | ((me // 4) == 2)
            kk = groups - k
            kk = jnp.where(inner & (kk >= 8), jnp.bitwise_xor(kk, 4), kk)
            action(jnp.bitwise_xor(me, kk))

    def tell(q):
        pl.semaphore_signal(barrier, inc=1, device_id=device(q, part), device_id_type=MESH)

    each(1, tell)
    for d in range(1, parts):
        pl.semaphore_signal(barrier, inc=1, device_id=device(me, sibling(d)), device_id_type=MESH)

    loads = [
        pltpu.make_async_copy(given, held, load_sem.at[i])
        for i, (given, held) in enumerate(((cid_in, cid_ref), (owner_in, owner_ref), (emb_in, emb_ref)))
    ]
    for load in loads:
        load.start()
    loads[0].wait()
    loads[1].wait()

    cid = cid_ref[...]
    cluster_hit = one_hot(iota((clusters_all, rows_here), 0) == cid)
    owner_cl = iota((groups, clusters_all), 0) == owner_ref[...]
    owner_cl_hot = one_hot(owner_cl)
    before_cl = one_hot(iota((clusters_all, clusters_all), 0) < iota((clusters_all, clusters_all), 1))
    local_rank = dot(owner_cl_hot, before_cl)
    label_cl = jnp.where(owner_cl, local_rank + 1.0, 0.0).astype(BF16)
    labels = dot(label_cl, cluster_hit)
    owner_hot = jnp.where(labels > 0.5, 1.0, 0.0)
    before = one_hot(iota((rows_here, rows_here), 0) < iota((rows_here, rows_here), 1))
    prefix = dot(owner_hot.astype(BF16), before)
    rank = jnp.sum(owner_hot * prefix, axis=0, keepdims=True).astype(jnp.int32)
    lane_hit = one_hot(iota((LANES, rows_here), 0) == rank + (me % per_row) * cap, F32)
    id_block = dot(labels.astype(BF16), lane_hit.astype(BF16), ((1,), (1,)))
    for g in range(groups):
        out_ids[g] = id_block[g : g + 1]
    label = jnp.sum(labels, axis=0, keepdims=True).astype(jnp.int32)
    local_hit = one_hot(iota((LANES, rows_here), 0) + 1 == label, F32)
    rank_hot = one_hot(iota((cap, rows_here), 0) == rank, F32)
    loads[2].wait()
    emb = emb_ref[...]
    per_step = max(1, 256 // cap)
    for g0 in range(0, groups, per_step):
        placed = jnp.concatenate(
            [(rank_hot * owner_hot[g : g + 1]).astype(BF16) for g in range(g0, min(g0 + per_step, groups))], axis=0
        )
        outgoing[g0 : g0 + per_step] = dot(placed, emb).astype(BF16).reshape(per_step, cap, width)

    def row_copy(to, frm):
        return pltpu.make_async_remote_copy(
            src_ref=outgoing.at[to], dst_ref=keys.at[part, me],
            send_sem=send_sem.at[to], recv_sem=recv_sem.at[frm],
            device_id=device(to, part), device_id_type=MESH,
        )

    def id_copy(to, frm):
        return pltpu.make_async_remote_copy(
            src_ref=out_ids.at[to], dst_ref=key_ids.at[part, me],
            send_sem=id_send.at[to], recv_sem=id_recv.at[frm],
            device_id=device(to, part), device_id_type=MESH,
        )

    def forward(q, piece, d, home):
        return pltpu.make_async_remote_copy(
            src_ref=keys.at[home, q], dst_ref=keys.at[home, q],
            send_sem=fwd_send.at[d, q], recv_sem=fwd_recv.at[home, q],
            device_id=device(me, piece), device_id_type=MESH,
        )

    def forward_ids(piece, d, home):
        return pltpu.make_async_remote_copy(
            src_ref=key_ids.at[home], dst_ref=key_ids.at[home],
            send_sem=idf_send.at[d], recv_sem=idf_recv.at[home],
            device_id=device(me, piece), device_id_type=MESH,
        )

    def send(q):
        id_copy(q, me).start()
        row_copy(q, me).start()

    pl.semaphore_wait(barrier, groups - 1 + parts - 1)
    each(1, lambda q: id_copy(q, me).start())
    each(1, lambda q: row_copy(q, me).start())

    own_rows = pltpu.make_async_copy(outgoing.at[me], keys.at[part, me], local_sem.at[0])
    own_ids = pltpu.make_async_copy(out_ids.at[me], key_ids.at[part, me], local_sem.at[1])
    own_rows.start()
    own_ids.start()
    own_rows.wait()
    own_ids.wait()
    for d in range(1, parts):
        forward(me, sibling(d), d, part).start()

    def take(q):
        row_copy(q, q).wait_recv()
        for d in range(1, parts):
            forward(q, sibling(d), d, part).start()

    @pl.loop(0, groups - 1, unroll=groups <= 16)
    def _(t):
        q = peer_in(t)
        id_copy(q, q).wait_recv()

    for d in range(1, parts):
        forward_ids(sibling(d), d, part).start()
    for d in range(1, parts):
        home = sibling(d)
        forward_ids(home, d, home).wait_recv()

    for piece in range(parts):
        for l in range(lane_rows):
            row = key_ids[piece, l * per_row]
            for j in range(1, per_row):
                row = row + key_ids[piece, l * per_row + j]
            id_rows[piece, l] = row
    query_rows = []
    for l in range(lane_rows):
        row = id_rows[part, l]
        query_rows.append(row)
        id_cols[l * LANES : (l + 1) * LANES] = jnp.transpose(jnp.broadcast_to(row, (LANES, LANES)))

    each(1, take)

    for d in range(1, parts):
        home = sibling(d)

        @pl.loop(0, groups, unroll=groups <= 16)
        def _(q):
            forward(q, home, d, home).wait_recv()

    scale = 1.0 / width**0.5
    chunk_groups = KEY_CHUNK // cap
    chunk_lanes = KEY_CHUNK // LANES
    per_piece = groups // chunk_groups
    n_chunks = parts * per_piece

    queries = keys[part].reshape(slots, width)
    id_col = jnp.concatenate([id_cols[...]] * chunk_lanes, axis=1)
    gap = iota((slots, KEY_CHUNK), 0) - iota((slots, KEY_CHUNK), 1)

    def score_chunk(j, high):
        piece, at = j // per_piece, j % per_piece
        block = keys[piece, pl.ds(at * chunk_groups, chunk_groups)].reshape(KEY_CHUNK, width)
        raw = dot(queries, block, ((1,), (1,))) * scale
        id_row = jnp.concatenate([id_rows[piece, at * chunk_lanes + i] for i in range(chunk_lanes)], axis=1)
        own_gap = (piece - part) * slots + at * KEY_CHUNK
        masked = jnp.where((id_col == id_row) & (gap != own_gap), raw, FLOOR_SCORE)
        scores[j] = masked
        folded = masked[:, :LANES]
        for i in range(1, chunk_lanes):
            folded = jnp.maximum(folded, masked[:, i * LANES : (i + 1) * LANES])
        return jnp.maximum(high, folded)

    high = lax.fori_loop(
        0, n_chunks, score_chunk, jnp.full((slots, LANES), FLOOR_SCORE, F32), unroll=n_chunks <= 4
    )
    highest = jnp.max(high, axis=1, keepdims=True)

    def sum_chunk(j, total):
        value = jnp.exp(scores[j] - highest)
        for i in range(chunk_lanes):
            total = total + value[:, i * LANES : (i + 1) * LANES]
        return total

    total = lax.fori_loop(0, n_chunks, sum_chunk, jnp.zeros((slots, LANES), F32), unroll=n_chunks <= 4)
    density = column_to_row(highest + jnp.log(jnp.sum(total, axis=1, keepdims=True)))
    labels_row = jnp.concatenate(query_rows, axis=1)
    member = labels_row == (iota((local_clusters, slots), 0) + 1).astype(F32)
    part_sum = jnp.sum(jnp.where(member, density, 0.0), axis=1, keepdims=True)
    part_count = jnp.sum(jnp.where(member, 1.0, 0.0), axis=1, keepdims=True)
    diagonal = iota((local_clusters, LANES), 0) == iota((local_clusters, LANES), 1)
    sum_row = jnp.sum(jnp.where(diagonal, part_sum, 0.0), axis=0, keepdims=True)
    count_row = jnp.sum(jnp.where(diagonal, part_count, 0.0), axis=0, keepdims=True)
    kept = jnp.where(labels_row > 0.5, density, 0.0)
    for l in range(lane_rows):
        result[l] = jnp.concatenate(
            [kept[:, l * LANES : (l + 1) * LANES], sum_row, count_row, count_row], axis=0
        )

    def ret_copy(to, piece, home, frm):
        return pltpu.make_async_remote_copy(
            src_ref=result.at[to // per_row], dst_ref=returned.at[part, me],
            send_sem=ret_send.at[piece, to], recv_sem=ret_recv.at[home, frm],
            device_id=device(to, piece), device_id_type=MESH,
        )

    def give(q):
        for d in range(parts):
            ret_copy(q, sibling(d), part, me).start()

    each(1, give)

    for d in range(1, parts):
        ret_copy(me, sibling(d), part, me).start()

    own_ret = pltpu.make_async_copy(result.at[me // per_row], returned.at[part, me], local_sem.at[2])
    own_ret.start()
    own_ret.wait()

    @pl.loop(0, groups - 1, unroll=groups <= 16)
    def _(t):
        q = peer_in(t)
        id_copy(q, q).wait_send()
        row_copy(q, q).wait_send()

    for d in range(1, parts):
        forward_ids(sibling(d), d, part).wait_send()

        @pl.loop(0, groups, unroll=groups <= 16)
        def _(q):
            forward(q, sibling(d), d, part).wait_send()

    @pl.loop(0, groups - 1, unroll=groups <= 16)
    def _(t):
        q = peer_in(t)
        for d in range(parts):
            ret_copy(q, sibling(d), sibling(d), q).wait_recv()

    for d in range(1, parts):
        ret_copy(me, sibling(d), sibling(d), me).wait_recv()

    back = jnp.concatenate([returned[part, g, 0:1] for g in range(groups)], axis=0)
    total_sum = jnp.concatenate([returned[0, g, 1:2] for g in range(groups)], axis=0)
    total_count = jnp.concatenate([returned[0, g, 2:3] for g in range(groups)], axis=0)
    for piece in range(1, parts):
        total_sum += jnp.concatenate([returned[piece, g, 1:2] for g in range(groups)], axis=0)
        total_count += jnp.concatenate([returned[piece, g, 2:3] for g in range(groups)], axis=0)
    mean = total_sum / jnp.maximum(total_count, 1.0)
    picked = dot(
        jnp.concatenate([back, -mean], axis=1),
        jnp.concatenate([lane_hit, local_hit], axis=0),
        precision=lax.Precision.HIGHEST,
    )
    out_ref[...] = jnp.sum(owner_hot * picked, axis=0)

    @pl.loop(0, groups - 1, unroll=groups <= 16)
    def _(t):
        q = peer_in(t)
        for d in range(parts):
            ret_copy(q, sibling(d), sibling(d), q).wait_send()

    for d in range(1, parts):
        ret_copy(me, sibling(d), sibling(d), me).wait_send()


def on_device(embeddings, cluster_id, owner_map):
    rows_here, width = embeddings.shape
    clusters_all = owner_map.shape[0]
    groups = lax.axis_size("rows")
    parts = lax.axis_size("split")
    cap = 2 * rows_here // groups
    slots = groups * cap
    lane_rows = slots // LANES
    local_clusters = clusters_all // groups
    dma = pltpu.SemaphoreType.DMA
    vmem = pl.BlockSpec(memory_space=pltpu.VMEM)
    out = pl.pallas_call(
        functools.partial(kernel, groups, parts, local_clusters),
        out_shape=jax.ShapeDtypeStruct((rows_here,), F32),
        in_specs=[pl.BlockSpec(memory_space=pl.ANY)] * 3,
        out_specs=vmem,
        scratch_shapes=[
            pltpu.VMEM((rows_here, width), BF16),
            pltpu.VMEM((1, rows_here), jnp.int32),
            pltpu.VMEM((1, clusters_all), jnp.int32),
            pltpu.VMEM((groups, cap, width), BF16),
            pltpu.VMEM((groups, 1, LANES), F32),
            pltpu.VMEM((parts, groups, cap, width), BF16),
            pltpu.VMEM((parts, groups, 1, LANES), F32),
            pltpu.VMEM((parts, lane_rows, 1, LANES), F32),
            pltpu.VMEM((slots, LANES), F32),
            pltpu.VMEM((parts * slots // KEY_CHUNK, slots, KEY_CHUNK), F32),
            pltpu.VMEM((lane_rows, 4, LANES), F32),
            pltpu.VMEM((parts, groups, 4, LANES), F32),
            dma((groups,)), dma((groups,)), dma((groups,)), dma((groups,)),
            dma((parts, groups)), dma((parts, groups)), dma((parts,)), dma((parts,)),
            dma((parts, groups)), dma((parts, groups)), dma((3,)),
            dma((3,)),
        ],
        compiler_params=pltpu.CompilerParams(
            collective_id=0, has_side_effects=True, vmem_limit_bytes=60 * 1024 * 1024
        ),
        name="soft_neighbour",
    )(embeddings, cluster_id.reshape(1, rows_here), owner_map.reshape(1, clusters_all))
    return out


def solution(mesh):
    placed = (P(("rows", "split"), None), P(("rows", "split")), P())
    return jax.shard_map(
        on_device, mesh=mesh, in_specs=placed, out_specs=P(("rows", "split")), check_vma=False
    )
```

```python
import functools
import math

import jax
import jax.numpy as jnp
from jax import lax
from jax.experimental import pallas as pl
from jax.experimental.pallas import tpu as pltpu
from jax.sharding import PartitionSpec as P

FLOOR_SCORE = -1e30
LANES = 128
SUBLANES = 8
MESH = pl.DeviceIdType.MESH
F32 = jnp.float32
BF16 = jnp.bfloat16


def iota(shape, dim):
    return lax.broadcasted_iota(jnp.int32, shape, dim)


def one_hot(hit, dtype=BF16):
    return jnp.where(hit, 1.0, 0.0).astype(dtype)


def dot(a, b, dims=((1,), (0,))):
    return lax.dot_general(a, b, (dims, ((), ())), preferred_element_type=F32)


def dot_transposed(a, b):
    return dot(a, b, ((1,), (1,)))


def kernel(
    groups, parts, local_clusters,
    emb_in, cid_in, owner_in, out_ref,
    emb_ref, cid_ref, owner_ref,
    outgoing, out_ids, keys, key_ids, id_rows, id_cols, result, returned,
    load_sem, row_send, row_recv, id_send, id_recv,
    fwd_send, fwd_recv, idf_send, idf_recv, ret_send, ret_recv,
):
    rows_here, width = emb_ref.shape
    clusters_all = owner_ref.shape[1]
    cap = outgoing.shape[1]
    per_class = LANES // cap
    classes = groups // per_class
    r, s = lax.axis_index("rows"), lax.axis_index("split")
    me = (r // parts) * parts + s
    part = r % parts
    level, place = me // per_class, me % per_class
    inner = (level > 0) & (level < classes - 1)

    def device(group, piece):
        return ((group // parts) * parts + piece, group % parts)

    def sibling(d):
        return (part + d) % parts

    def class_at(step):
        outer_step, inner_step = step
        if outer_step == inner_step:
            return jnp.bitwise_xor(level, outer_step)
        return jnp.bitwise_xor(level, jnp.where(inner, inner_step, outer_step))

    def peers(step):
        near = step == (0, 0)
        start = class_at(step) * per_class
        return [start + jnp.bitwise_xor(place, j) for j in reversed(range(1 if near else 0, per_class))]

    if classes == 4:
        farthest_first = [(3, 2), (2, 3), (1, 1), (0, 0)]
        arriving = [(0, 0), (3, 2), (1, 1), (2, 3)]
    else:
        farthest_first = [(k, k) for k in reversed(range(classes))]
        arriving = [(k, k) for k in range(classes)]
    others = [q for step in farthest_first for q in peers(step)]

    loads = [
        pltpu.make_async_copy(given, held, load_sem.at[i])
        for i, (given, held) in enumerate(((cid_in, cid_ref), (owner_in, owner_ref), (emb_in, emb_ref)))
    ]
    for load in loads:
        load.start()

    barrier = pltpu.get_barrier_semaphore()
    for q in others:
        pl.semaphore_signal(barrier, inc=1, device_id=device(q, part), device_id_type=MESH)
    for d in range(1, parts):
        pl.semaphore_signal(barrier, inc=1, device_id=device(me, sibling(d)), device_id_type=MESH)

    before = one_hot(iota((rows_here, rows_here), 0) < iota((rows_here, rows_here), 1))
    before_cl = one_hot(iota((clusters_all, clusters_all), 0) < iota((clusters_all, clusters_all), 1))
    loads[0].wait()
    loads[1].wait()
    cid = cid_ref[...]
    cluster_hit = one_hot(iota((clusters_all, rows_here), 0) == cid)
    owner_cl = iota((groups, clusters_all), 0) == owner_ref[...]
    local_rank = dot(one_hot(owner_cl), before_cl)
    label_cl = jnp.where(owner_cl, local_rank + 1.0, 0.0).astype(BF16)
    labels = dot(label_cl, cluster_hit)
    owner_hot = jnp.where(labels > 0.5, 1.0, 0.0)
    prefix = dot(owner_hot.astype(BF16), before)
    rank = jnp.sum(owner_hot * prefix, axis=0, keepdims=True).astype(jnp.int32)
    lane_hit = one_hot(iota((LANES, rows_here), 0) == rank + place * cap)
    id_block = dot_transposed(labels.astype(BF16), lane_hit)
    for g in range(groups):
        out_ids[g] = id_block[g : g + 1]
    label = jnp.sum(labels, axis=0, keepdims=True).astype(jnp.int32)
    local_hit = one_hot(iota((LANES, rows_here), 0) + 1 == label)
    rank_hot = one_hot(iota((cap, rows_here), 0) == rank, F32)
    loads[2].wait()
    emb = emb_ref[...]
    per_step = max(1, 256 // cap)
    for g0 in range(0, groups, per_step):
        placed = jnp.concatenate(
            [(rank_hot * owner_hot[g : g + 1]).astype(BF16) for g in range(g0, min(g0 + per_step, groups))], axis=0
        )
        outgoing[g0 : g0 + per_step] = dot(placed, emb).astype(BF16).reshape(per_step, cap, width)

    def row_copy(to, frm):
        return pltpu.make_async_remote_copy(
            src_ref=outgoing.at[to], dst_ref=keys.at[part, me],
            send_sem=row_send.at[0], recv_sem=row_recv.at[frm],
            device_id=device(to, part), device_id_type=MESH,
        )

    def id_copy(to):
        return pltpu.make_async_remote_copy(
            src_ref=out_ids.at[to], dst_ref=key_ids.at[part, me],
            send_sem=id_send.at[0], recv_sem=id_recv.at[0],
            device_id=device(to, part), device_id_type=MESH,
        )

    def forward(src, q, d, home):
        return pltpu.make_async_remote_copy(
            src_ref=src, dst_ref=keys.at[home, q],
            send_sem=fwd_send.at[d], recv_sem=fwd_recv.at[home, q // per_class],
            device_id=device(me, sibling(d)), device_id_type=MESH,
        )

    def forward_ids(d, home):
        return pltpu.make_async_remote_copy(
            src_ref=key_ids.at[home], dst_ref=key_ids.at[home],
            send_sem=idf_send.at[d], recv_sem=idf_recv.at[home],
            device_id=device(me, sibling(d)), device_id_type=MESH,
        )

    def received(sem, ref):
        pltpu.make_async_copy(ref, ref, sem).wait()

    pl.semaphore_wait(barrier, groups - 1 + parts - 1)
    for q in others:
        id_copy(q).start()
    for q in others:
        row_copy(q, me).start()
    for d in range(1, parts):
        forward(outgoing.at[me], me, d, part).start()
    keys[part, me] = outgoing[me]
    key_ids[part, me] = out_ids[me]

    def take(step):
        for q in peers(step):
            row_copy(q, q).wait_recv()
            for d in range(1, parts):
                forward(keys.at[part, q], q, d, part).start()

    def class_rows(piece, c):
        return pl.ds(c * per_class, per_class)

    def take_forwarded(home, step):
        c = class_at(step)
        received(fwd_recv.at[home, c], keys.at[home, class_rows(home, c)])

    def read_ids(piece):
        for c in range(classes):
            row = key_ids[piece, c * per_class]
            for j in range(1, per_class):
                row = row + key_ids[piece, c * per_class + j]
            id_cols[piece, c] = jnp.transpose(jnp.broadcast_to(row, (LANES, LANES)))
            yield row

    take(arriving[0])
    received(id_recv.at[0], key_ids.at[part, pl.ds(0, groups - 1)])
    for d in range(1, parts):
        forward_ids(d, part).start()
    for c, row in enumerate(read_ids(part)):
        id_rows[c] = row
    take(arriving[1])
    for d in range(1, parts):
        home = sibling(d)
        received(idf_recv.at[home], key_ids.at[home])
        for _ in read_ids(home):
            pass
    for step in arriving[2:-1]:
        take(step)

    scale = 1.0 / math.sqrt(width)
    to_base_2 = scale / math.log(2.0)
    eye = iota((LANES, LANES), 0) == iota((LANES, LANES), 1)
    last, old = arriving[-1], arriving[:-1]

    def block(piece, step):
        return keys[piece, class_rows(piece, class_at(step))].reshape(LANES, width)

    def masked(raw, piece, key_step, query_step, own):
        hit = id_cols[piece, class_at(key_step)] == id_rows[class_at(query_step)]
        if own and key_step == query_step:
            hit = hit & jnp.logical_not(eye)
        return jnp.where(hit, raw, FLOOR_SCORE).reshape(LANES // SUBLANES, SUBLANES, LANES)

    def weigh(x):
        return jnp.exp2(x * to_base_2)

    def summed(tiles):
        high = functools.reduce(jnp.maximum, [jnp.max(t, axis=0) for t in tiles])
        total = functools.reduce(jnp.add, [jnp.sum(weigh(t - high[None]), axis=0) for t in tiles])
        return high, total

    def merged(a, b):
        high = jnp.maximum(a[0], b[0])
        return high, a[1] * weigh(a[0] - high) + b[1] * weigh(b[0] - high)

    def scored(piece, key_step, queries, query_steps, own):
        raw = dot_transposed(block(piece, key_step), queries)
        return [
            masked(raw[:, i * LANES : (i + 1) * LANES], piece, key_step, step, own)
            for i, step in enumerate(query_steps)
        ]

    for d in range(1, parts):
        for step in old:
            take_forwarded(sibling(d), step)
    old_queries = jnp.concatenate([block(part, step) for step in old], axis=0)
    stats = None
    for d in range(parts):
        for key_step in old:
            tiles = scored(sibling(d), key_step, old_queries, old, d == 0)
            fresh = [summed([t]) for t in tiles]
            stats = fresh if stats is None else [merged(a, b) for a, b in zip(stats, fresh)]

    diagonal = iota((local_clusters, LANES), 0) == iota((local_clusters, LANES), 1)
    cluster_label = (iota((local_clusters, LANES), 0) + 1).astype(F32)

    def spread(column):
        return jnp.sum(jnp.where(diagonal, column, 0.0), axis=0, keepdims=True)

    members = jnp.zeros((local_clusters, LANES), F32)
    for c in range(classes):
        members = members + jnp.where(id_rows[c] == cluster_label, 1.0, 0.0)
    count_row = spread(jnp.sum(members, axis=1, keepdims=True))

    take(last)
    all_steps = old + [last]
    queries = jnp.concatenate([block(part, step) for step in all_steps], axis=0)
    last_queries = block(part, last)
    fresh = [summed([t]) for t in scored(part, last, queries, all_steps, True)]
    for d in range(parts):
        for key_step in old:
            fresh[-1] = merged(
                fresh[-1], summed(scored(sibling(d), key_step, last_queries, [last], d == 0))
            )
    stats = [merged(a, b) for a, b in zip(stats, fresh)] + [fresh[-1]]
    for d in range(1, parts):
        take_forwarded(sibling(d), last)
        fresh = [summed([t]) for t in scored(sibling(d), last, queries, all_steps, False)]
        stats = [merged(a, b) for a, b in zip(stats, fresh)]

    cluster_sum = jnp.zeros((local_clusters, LANES), F32)
    kept = []
    for step, (high, total) in zip(all_steps, stats):
        highest = jnp.max(high, axis=0, keepdims=True)
        total = jnp.sum(total * weigh(high - highest), axis=0, keepdims=True)
        density = highest * scale + jnp.log(total)
        id_row = id_rows[class_at(step)]
        kept.append(jnp.where(id_row > 0.5, density, 0.0))
        cluster_sum = cluster_sum + jnp.where(id_row == cluster_label, density, 0.0)
    sum_row = spread(jnp.sum(cluster_sum, axis=1, keepdims=True))
    for step, row in zip(all_steps, kept):
        result[class_at(step)] = jnp.concatenate([row, sum_row, count_row, count_row], axis=0)

    def ret_copy(to, d):
        return pltpu.make_async_remote_copy(
            src_ref=result.at[to // per_class], dst_ref=returned.at[part * groups + me],
            send_sem=ret_send.at[0], recv_sem=ret_recv.at[0],
            device_id=device(to, sibling(d)), device_id_type=MESH,
        )

    for q in others:
        for d in range(parts):
            ret_copy(q, d).start()
    for d in range(1, parts):
        ret_copy(me, d).start()
    returned[part * groups + me] = result[level]

    received(row_send.at[0], outgoing.at[pl.ds(0, groups - 1)])
    received(id_send.at[0], out_ids.at[pl.ds(0, groups - 1)])
    for d in range(1, parts):
        received(fwd_send.at[d], outgoing)
        received(idf_send.at[d], out_ids)

    received(ret_recv.at[0], returned.at[pl.ds(0, parts * groups - 1)])
    back = jnp.concatenate([returned[part * groups + g, 0:1] for g in range(groups)], axis=0)
    totals = [
        functools.reduce(jnp.add, [
            jnp.concatenate([returned[piece * groups + g, at : at + 1] for g in range(groups)], axis=0)
            for piece in range(parts)
        ])
        for at in (1, 2)
    ]
    mean = totals[0] / jnp.maximum(totals[1], 1.0)
    left = jnp.concatenate([back, -mean], axis=1)
    pieces = []
    for _ in range(3):
        rounded = left.astype(BF16)
        pieces.append(rounded)
        left = left - rounded.astype(F32)
    picked = dot(jnp.concatenate(pieces, axis=0), jnp.concatenate([lane_hit, local_hit], axis=0))
    picked = picked[:groups] + (picked[groups : 2 * groups] + picked[2 * groups :])
    out_ref[...] = jnp.sum(owner_hot * picked, axis=0)
    received(ret_send.at[0], returned.at[pl.ds(0, parts * groups - 1)])


def on_device(embeddings, cluster_id, owner_map):
    rows_here, width = embeddings.shape
    clusters_all = owner_map.shape[0]
    groups = lax.axis_size("rows")
    parts = lax.axis_size("split")
    cap = 2 * rows_here // groups
    classes = groups * cap // LANES
    local_clusters = clusters_all // groups
    dma = pltpu.SemaphoreType.DMA
    return pl.pallas_call(
        functools.partial(kernel, groups, parts, local_clusters),
        out_shape=jax.ShapeDtypeStruct((rows_here,), F32),
        in_specs=[pl.BlockSpec(memory_space=pl.ANY)] * 3,
        out_specs=pl.BlockSpec(memory_space=pltpu.VMEM),
        scratch_shapes=[
            pltpu.VMEM((rows_here, width), BF16),
            pltpu.VMEM((1, rows_here), jnp.int32),
            pltpu.VMEM((1, clusters_all), jnp.int32),
            pltpu.VMEM((groups, cap, width), BF16),
            pltpu.VMEM((groups, 1, LANES), F32),
            pltpu.VMEM((parts, groups, cap, width), BF16),
            pltpu.VMEM((parts, groups, 1, LANES), F32),
            pltpu.VMEM((classes, 1, LANES), F32),
            pltpu.VMEM((parts, classes, LANES, LANES), F32),
            pltpu.VMEM((classes, 4, LANES), F32),
            pltpu.VMEM((parts * groups, 4, LANES), F32),
            dma((3,)), dma((1,)), dma((groups,)), dma((1,)), dma((1,)),
            dma((parts,)), dma((parts, classes)), dma((parts,)), dma((parts,)), dma((1,)), dma((1,)),
        ],
        compiler_params=pltpu.CompilerParams(
            collective_id=0, has_side_effects=True, vmem_limit_bytes=60 * 1024 * 1024
        ),
        name="soft_neighbour",
    )(embeddings, cluster_id.reshape(1, rows_here), owner_map.reshape(1, clusters_all))


def solution(mesh):
    placed = (P(("rows", "split"), None), P(("rows", "split")), P())
    return jax.shard_map(
        on_device, mesh=mesh, in_specs=placed, out_specs=P(("rows", "split")), check_vma=False
    )
```

```python
import functools
import math

import jax
import jax.numpy as jnp
from jax import lax
from jax.experimental import pallas as pl
from jax.experimental.pallas import tpu as pltpu
from jax.sharding import PartitionSpec as P

FLOOR_SCORE = -1e30
LANES = 128
SUBLANES = 8
MESH = pl.DeviceIdType.MESH
F32 = jnp.float32
BF16 = jnp.bfloat16


def iota(shape, dim):
    return lax.broadcasted_iota(jnp.int32, shape, dim)


def one_hot(hit, dtype=BF16):
    return jnp.where(hit, 1.0, 0.0).astype(dtype)


def dot(a, b, dims=((1,), (0,))):
    return lax.dot_general(a, b, (dims, ((), ())), preferred_element_type=F32)


def dot_transposed(a, b):
    return dot(a, b, ((1,), (1,)))


def kernel(
    groups, parts, local_clusters,
    emb_in, cid_in, owner_in, out_ref,
    emb_ref, cid_ref, owner_ref,
    outgoing, out_ids, keys, key_ids, id_rows, id_cols, result, returned,
    load_sem, row_send, row_recv, id_send, id_recv,
    fwd_send, fwd_recv, idf_send, idf_recv, ret_send, ret_recv, ready,
):
    rows_here, width = emb_ref.shape
    clusters_all = owner_ref.shape[1]
    cap = outgoing.shape[1]
    per_class = LANES // cap
    classes = groups // per_class
    r, s = lax.axis_index("rows"), lax.axis_index("split")
    me = (r // parts) * parts + s
    part = r % parts
    level, place = me // per_class, me % per_class
    inner = (level > 0) & (level < classes - 1)

    def device(group, piece):
        return ((group // parts) * parts + piece, group % parts)

    def sibling(d):
        return (part + d) % parts

    def class_at(step):
        outer_step, inner_step = step
        if outer_step == inner_step:
            return jnp.bitwise_xor(level, outer_step)
        return jnp.bitwise_xor(level, jnp.where(inner, inner_step, outer_step))

    def peers(step):
        near = step == (0, 0)
        start = class_at(step) * per_class
        return [start + jnp.bitwise_xor(place, j) for j in reversed(range(1 if near else 0, per_class))]

    if classes == 4:
        farthest_first = [(3, 2), (2, 3), (1, 1), (0, 0)]
        arriving = [(0, 0), (3, 2), (1, 1), (2, 3)]
    else:
        farthest_first = [(k, k) for k in reversed(range(classes))]
        arriving = [(k, k) for k in range(classes)]
    others = [q for step in farthest_first for q in peers(step)]

    loads = [
        pltpu.make_async_copy(given, held, load_sem.at[i])
        for i, (given, held) in enumerate(((cid_in, cid_ref), (owner_in, owner_ref), (emb_in, emb_ref)))
    ]
    for load in loads:
        load.start()

    barrier = pltpu.get_barrier_semaphore()

    def tell(semaphore, q):
        pl.semaphore_signal(semaphore, inc=1, device_id=device(q, part), device_id_type=MESH)

    beside = peers((0, 0))
    beyond = [q for step in farthest_first[:-1] for q in peers(step)]
    late = level == classes - 1

    @pl.when(jnp.logical_not(late))
    def _():
        for q in beyond:
            tell(barrier, q)

    for q in beside:
        tell(barrier, q)
    for d in range(1, parts):
        pl.semaphore_signal(barrier, inc=1, device_id=device(me, sibling(d)), device_id_type=MESH)

    before = one_hot(iota((rows_here, rows_here), 0) < iota((rows_here, rows_here), 1))
    before_cl = one_hot(iota((clusters_all, clusters_all), 0) < iota((clusters_all, clusters_all), 1))
    loads[0].wait()
    loads[1].wait()
    cid = cid_ref[...]
    cluster_hit = one_hot(iota((clusters_all, rows_here), 0) == cid)
    owner_cl = iota((groups, clusters_all), 0) == owner_ref[...]
    local_rank = dot(one_hot(owner_cl), before_cl)
    label_cl = jnp.where(owner_cl, local_rank + 1.0, 0.0).astype(BF16)
    labels = dot(label_cl, cluster_hit)
    owner_hot = jnp.where(labels > 0.5, 1.0, 0.0)
    prefix = dot(owner_hot.astype(BF16), before)
    rank = jnp.sum(owner_hot * prefix, axis=0, keepdims=True).astype(jnp.int32)
    lane_hit = one_hot(iota((LANES, rows_here), 0) == rank + place * cap)
    id_block = dot_transposed(labels.astype(BF16), lane_hit)
    for g in range(groups):
        out_ids[g] = id_block[g : g + 1]
    label = jnp.sum(labels, axis=0, keepdims=True).astype(jnp.int32)
    local_hit = one_hot(iota((LANES, rows_here), 0) + 1 == label)
    rank_hot = one_hot(iota((cap, rows_here), 0) == rank, F32)
    loads[2].wait()
    emb = emb_ref[...]
    per_step = max(1, 256 // cap)
    for g0 in range(0, groups, per_step):
        placed = jnp.concatenate(
            [(rank_hot * owner_hot[g : g + 1]).astype(BF16) for g in range(g0, min(g0 + per_step, groups))], axis=0
        )
        outgoing[g0 : g0 + per_step] = dot(placed, emb).astype(BF16).reshape(per_step, cap, width)

    def row_copy(to, frm):
        return pltpu.make_async_remote_copy(
            src_ref=outgoing.at[to], dst_ref=keys.at[part, me],
            send_sem=row_send.at[0], recv_sem=row_recv.at[frm],
            device_id=device(to, part), device_id_type=MESH,
        )

    def id_copy(to):
        return pltpu.make_async_remote_copy(
            src_ref=out_ids.at[to], dst_ref=key_ids.at[part, me],
            send_sem=id_send.at[0], recv_sem=id_recv.at[0],
            device_id=device(to, part), device_id_type=MESH,
        )

    def forward(src, q, d, home):
        return pltpu.make_async_remote_copy(
            src_ref=src, dst_ref=keys.at[home, q],
            send_sem=fwd_send.at[d], recv_sem=fwd_recv.at[home, q // per_class],
            device_id=device(me, sibling(d)), device_id_type=MESH,
        )

    def forward_ids(d, home):
        return pltpu.make_async_remote_copy(
            src_ref=key_ids.at[home], dst_ref=key_ids.at[home],
            send_sem=idf_send.at[d], recv_sem=idf_recv.at[home],
            device_id=device(me, sibling(d)), device_id_type=MESH,
        )

    def received(sem, ref):
        pltpu.make_async_copy(ref, ref, sem).wait()

    def send(step, ids=True, rows=True, chosen=slice(None)):
        if ids:
            for q in peers(step):
                id_copy(q).start()
        if rows:
            for q in peers(step)[chosen]:
                row_copy(q, me).start()

    pl.semaphore_wait(barrier, groups - 1 + parts - 1 - jnp.where(late, 0, per_class))

    @pl.when(late)
    def _():
        for q in beyond:
            tell(ready, q)

    half = per_class // 2
    outward, inward, nearby, same = farthest_first

    @pl.when(level < classes // 2)
    def _():
        send(inward, rows=False)
        send(same, rows=False)
        send(nearby, rows=False)
        send(inward, ids=False, chosen=slice(0, 2))

        @pl.when(level == 0)
        def _():
            send(inward, ids=False, chosen=slice(2, 4))

        send(same, ids=False)
        pl.semaphore_wait(ready, per_class)
        send(outward)
        send(nearby, ids=False)

        @pl.when(level == 0)
        def _():
            send(inward, ids=False, chosen=slice(4, None))

        @pl.when(level == 1)
        def _():
            send(inward, ids=False, chosen=slice(2, None))

    @pl.when(level >= classes // 2)
    def _():
        for step in (outward, inward, same, nearby):
            if step == nearby:
                @pl.when(jnp.logical_not(late))
                def _():
                    pl.semaphore_wait(ready, per_class)
            if step == outward:
                send(inward, rows=False)
                send(same, rows=False)
            send(step, ids=step in (outward, nearby))

    for d in range(1, parts):
        forward(outgoing.at[me], me, d, part).start()
    keys[part, me] = outgoing[me]
    key_ids[part, me] = out_ids[me]

    def take(step):
        for q in peers(step):
            row_copy(q, q).wait_recv()
            for d in range(1, parts):
                forward(keys.at[part, q], q, d, part).start()

    def class_rows(piece, c):
        return pl.ds(c * per_class, per_class)

    def take_forwarded(home, step):
        c = class_at(step)
        received(fwd_recv.at[home, c], keys.at[home, class_rows(home, c)])

    def read_ids(piece):
        for c in range(classes):
            row = key_ids[piece, c * per_class]
            for j in range(1, per_class):
                row = row + key_ids[piece, c * per_class + j]
            id_cols[piece, c] = jnp.transpose(jnp.broadcast_to(row, (LANES, LANES)))
            yield row

    take(arriving[0])
    received(id_recv.at[0], key_ids.at[part, pl.ds(0, groups - 1)])
    for d in range(1, parts):
        forward_ids(d, part).start()
    for c, row in enumerate(read_ids(part)):
        id_rows[c] = row
    take(arriving[1])
    for d in range(1, parts):
        home = sibling(d)
        received(idf_recv.at[home], key_ids.at[home])
        for _ in read_ids(home):
            pass
    for step in arriving[2:-1]:
        take(step)

    scale = 1.0 / math.sqrt(width)
    to_base_2 = scale / math.log(2.0)
    eye = iota((LANES, LANES), 0) == iota((LANES, LANES), 1)
    last, old = arriving[-1], arriving[:-1]

    def block(piece, step):
        return keys[piece, class_rows(piece, class_at(step))].reshape(LANES, width)

    def masked(raw, piece, key_step, query_step, own):
        hit = id_cols[piece, class_at(key_step)] == id_rows[class_at(query_step)]
        if own and key_step == query_step:
            hit = hit & jnp.logical_not(eye)
        return jnp.where(hit, raw, FLOOR_SCORE).reshape(LANES // SUBLANES, SUBLANES, LANES)

    def weigh(x):
        return jnp.exp2(x * to_base_2)

    def summed(tiles):
        high = functools.reduce(jnp.maximum, [jnp.max(t, axis=0) for t in tiles])
        total = functools.reduce(jnp.add, [jnp.sum(weigh(t - high[None]), axis=0) for t in tiles])
        return high, total

    def merged(a, b):
        high = jnp.maximum(a[0], b[0])
        return high, a[1] * weigh(a[0] - high) + b[1] * weigh(b[0] - high)

    def scored(piece, key_step, queries, query_steps, own):
        raw = dot_transposed(block(piece, key_step), queries)
        return [
            masked(raw[:, i * LANES : (i + 1) * LANES], piece, key_step, step, own)
            for i, step in enumerate(query_steps)
        ]

    for d in range(1, parts):
        for step in old:
            take_forwarded(sibling(d), step)
    old_queries = jnp.concatenate([block(part, step) for step in old], axis=0)
    stats = None
    for d in range(parts):
        for key_step in old:
            tiles = scored(sibling(d), key_step, old_queries, old, d == 0)
            fresh = [summed([t]) for t in tiles]
            stats = fresh if stats is None else [merged(a, b) for a, b in zip(stats, fresh)]

    diagonal = iota((local_clusters, LANES), 0) == iota((local_clusters, LANES), 1)
    cluster_label = (iota((local_clusters, LANES), 0) + 1).astype(F32)

    def spread(column):
        return jnp.sum(jnp.where(diagonal, column, 0.0), axis=0, keepdims=True)

    members = jnp.zeros((local_clusters, LANES), F32)
    for c in range(classes):
        members = members + jnp.where(id_rows[c] == cluster_label, 1.0, 0.0)
    count_row = spread(jnp.sum(members, axis=1, keepdims=True))

    take(last)
    all_steps = old + [last]
    queries = jnp.concatenate([block(part, step) for step in all_steps], axis=0)
    last_queries = block(part, last)
    fresh = [summed([t]) for t in scored(part, last, queries, all_steps, True)]
    for d in range(parts):
        for key_step in old:
            fresh[-1] = merged(
                fresh[-1], summed(scored(sibling(d), key_step, last_queries, [last], d == 0))
            )
    stats = [merged(a, b) for a, b in zip(stats, fresh)] + [fresh[-1]]
    for d in range(1, parts):
        take_forwarded(sibling(d), last)
        fresh = [summed([t]) for t in scored(sibling(d), last, queries, all_steps, False)]
        stats = [merged(a, b) for a, b in zip(stats, fresh)]

    cluster_sum = jnp.zeros((local_clusters, LANES), F32)
    kept = []
    for step, (high, total) in zip(all_steps, stats):
        highest = jnp.max(high, axis=0, keepdims=True)
        total = jnp.sum(total * weigh(high - highest), axis=0, keepdims=True)
        density = highest * scale + jnp.log(total)
        id_row = id_rows[class_at(step)]
        kept.append(jnp.where(id_row > 0.5, density, 0.0))
        cluster_sum = cluster_sum + jnp.where(id_row == cluster_label, density, 0.0)
    sum_row = spread(jnp.sum(cluster_sum, axis=1, keepdims=True))
    for step, row in zip(all_steps, kept):
        result[class_at(step)] = jnp.concatenate([row, sum_row, count_row, count_row], axis=0)

    def ret_copy(to, d):
        return pltpu.make_async_remote_copy(
            src_ref=result.at[to // per_class], dst_ref=returned.at[part * groups + me],
            send_sem=ret_send.at[0], recv_sem=ret_recv.at[0],
            device_id=device(to, sibling(d)), device_id_type=MESH,
        )

    for q in others:
        for d in range(parts):
            ret_copy(q, d).start()
    for d in range(1, parts):
        ret_copy(me, d).start()
    returned[part * groups + me] = result[level]

    received(row_send.at[0], outgoing.at[pl.ds(0, groups - 1)])
    received(id_send.at[0], out_ids.at[pl.ds(0, groups - 1)])
    for d in range(1, parts):
        received(fwd_send.at[d], outgoing)
        received(idf_send.at[d], out_ids)

    received(ret_recv.at[0], returned.at[pl.ds(0, parts * groups - 1)])
    back = jnp.concatenate([returned[part * groups + g, 0:1] for g in range(groups)], axis=0)
    totals = [
        functools.reduce(jnp.add, [
            jnp.concatenate([returned[piece * groups + g, at : at + 1] for g in range(groups)], axis=0)
            for piece in range(parts)
        ])
        for at in (1, 2)
    ]
    mean = totals[0] / jnp.maximum(totals[1], 1.0)
    left = jnp.concatenate([back, -mean], axis=1)
    pieces = []
    for _ in range(3):
        rounded = left.astype(BF16)
        pieces.append(rounded)
        left = left - rounded.astype(F32)
    picked = dot(jnp.concatenate(pieces, axis=0), jnp.concatenate([lane_hit, local_hit], axis=0))
    picked = picked[:groups] + (picked[groups : 2 * groups] + picked[2 * groups :])
    out_ref[...] = jnp.sum(owner_hot * picked, axis=0)
    received(ret_send.at[0], returned.at[pl.ds(0, parts * groups - 1)])


def on_device(embeddings, cluster_id, owner_map):
    rows_here, width = embeddings.shape
    clusters_all = owner_map.shape[0]
    groups = lax.axis_size("rows")
    parts = lax.axis_size("split")
    cap = 2 * rows_here // groups
    classes = groups * cap // LANES
    local_clusters = clusters_all // groups
    dma = pltpu.SemaphoreType.DMA
    return pl.pallas_call(
        functools.partial(kernel, groups, parts, local_clusters),
        out_shape=pltpu.VMEM((rows_here,), F32),
        in_specs=[pl.BlockSpec(memory_space=pl.ANY)] * 3,
        out_specs=pl.BlockSpec(memory_space=pltpu.VMEM),
        scratch_shapes=[
            pltpu.VMEM((rows_here, width), BF16),
            pltpu.VMEM((1, rows_here), jnp.int32),
            pltpu.VMEM((1, clusters_all), jnp.int32),
            pltpu.VMEM((groups, cap, width), BF16),
            pltpu.VMEM((groups, 1, LANES), F32),
            pltpu.VMEM((parts, groups, cap, width), BF16),
            pltpu.VMEM((parts, groups, 1, LANES), F32),
            pltpu.VMEM((classes, 1, LANES), F32),
            pltpu.VMEM((parts, classes, LANES, LANES), F32),
            pltpu.VMEM((classes, 4, LANES), F32),
            pltpu.VMEM((parts * groups, 4, LANES), F32),
            dma((3,)), dma((1,)), dma((groups,)), dma((1,)), dma((1,)),
            dma((parts,)), dma((parts, classes)), dma((parts,)), dma((parts,)), dma((1,)), dma((1,)),
            pltpu.SemaphoreType.REGULAR,
        ],
        compiler_params=pltpu.CompilerParams(
            collective_id=0, has_side_effects=True, vmem_limit_bytes=60 * 1024 * 1024
        ),
        name="soft_neighbour",
    )(embeddings, cluster_id.reshape(1, rows_here), owner_map.reshape(1, clusters_all))


def solution(mesh):
    placed = (P(("rows", "split"), None), P(("rows", "split")), P())
    return jax.shard_map(
        on_device, mesh=mesh, in_specs=placed, out_specs=P(("rows", "split")), check_vma=False
    )
```

```python
import functools
import math

import jax
import jax.numpy as jnp
from jax import lax
from jax.experimental import pallas as pl
from jax.experimental.pallas import tpu as pltpu
from jax.sharding import PartitionSpec as P

FLOOR_SCORE = -1e30
LANES = 128
SUBLANES = 8
MESH = pl.DeviceIdType.MESH
F32 = jnp.float32
BF16 = jnp.bfloat16


def iota(shape, dim):
    return lax.broadcasted_iota(jnp.int32, shape, dim)


def one_hot(hit, dtype=BF16):
    return jnp.where(hit, 1.0, 0.0).astype(dtype)


def dot(a, b, dims=((1,), (0,))):
    return lax.dot_general(a, b, (dims, ((), ())), preferred_element_type=F32)


def dot_transposed(a, b):
    return dot(a, b, ((1,), (1,)))


def kernel(
    groups, parts, local_clusters,
    emb_in, cid_in, owner_in, out_ref,
    emb_ref, cid_ref, owner_ref,
    outgoing, out_ids, keys, key_ids, id_rows, id_cols, result, returned,
    load_sem, row_send, row_recv, id_send, id_recv,
    fwd_send, fwd_recv, idf_send, idf_recv, ret_send, ret_recv, ready,
):
    rows_here, width = emb_ref.shape
    clusters_all = owner_ref.shape[1]
    cap = outgoing.shape[1]
    per_class = LANES // cap
    classes = groups // per_class
    r, s = lax.axis_index("rows"), lax.axis_index("split")
    me = (r // parts) * parts + s
    part = r % parts
    level, place = me // per_class, me % per_class
    half = per_class // 2
    inner = (level > 0) & (level < classes - 1)

    def device(group, piece):
        return ((group // parts) * parts + piece, group % parts)

    def sibling(d):
        return (part + d) % parts

    def class_at(step):
        outer_step, inner_step = step
        if outer_step == inner_step:
            return jnp.bitwise_xor(level, outer_step)
        return jnp.bitwise_xor(level, jnp.where(inner, inner_step, outer_step))

    def peers(step):
        near = step == (0, 0)
        start = class_at(step) * per_class
        return [start + jnp.bitwise_xor(place, j) for j in reversed(range(1 if near else 0, per_class))]

    if classes == 4:
        farthest_first = [(3, 2), (2, 3), (1, 1), (0, 0)]
        arriving = [(0, 0), (3, 2), (1, 1), (2, 3)]
    else:
        farthest_first = [(k, k) for k in reversed(range(classes))]
        arriving = [(k, k) for k in range(classes)]
    last, old = arriving[-1], arriving[:-1]
    others = [q for step in farthest_first for q in peers(step)]

    loads = [
        pltpu.make_async_copy(given, held, load_sem.at[i])
        for i, (given, held) in enumerate(((cid_in, cid_ref), (owner_in, owner_ref), (emb_in, emb_ref)))
    ]
    for load in loads:
        load.start()

    barrier = pltpu.get_barrier_semaphore()

    def tell(semaphore, q):
        pl.semaphore_signal(semaphore, inc=1, device_id=device(q, part), device_id_type=MESH)

    beside = peers((0, 0))
    beyond = [q for step in farthest_first[:-1] for q in peers(step)]
    late = level == classes - 1

    @pl.when(jnp.logical_not(late))
    def _():
        for q in beyond:
            tell(barrier, q)

    for q in beside:
        tell(barrier, q)
    for d in range(1, parts):
        pl.semaphore_signal(barrier, inc=1, device_id=device(me, sibling(d)), device_id_type=MESH)

    before = one_hot(iota((rows_here, rows_here), 0) < iota((rows_here, rows_here), 1))
    before_cl = one_hot(iota((clusters_all, clusters_all), 0) < iota((clusters_all, clusters_all), 1))
    loads[0].wait()
    loads[1].wait()
    cid = cid_ref[...]
    cluster_hit = one_hot(iota((clusters_all, rows_here), 0) == cid)
    owner_cl = iota((groups, clusters_all), 0) == owner_ref[...]
    local_rank = dot(one_hot(owner_cl), before_cl)
    label_cl = jnp.where(owner_cl, local_rank + 1.0, 0.0).astype(BF16)
    labels = dot(label_cl, cluster_hit)
    owner_hot = jnp.where(labels > 0.5, 1.0, 0.0)
    prefix = dot(owner_hot.astype(BF16), before)
    rank = jnp.sum(owner_hot * prefix, axis=0, keepdims=True).astype(jnp.int32)
    lane_hit = one_hot(iota((LANES, rows_here), 0) == rank + place * cap)
    id_block = dot_transposed(labels.astype(BF16), lane_hit)
    for g in range(groups):
        out_ids[g] = id_block[g : g + 1]
    label = jnp.sum(labels, axis=0, keepdims=True).astype(jnp.int32)
    local_hit = one_hot(iota((LANES, rows_here), 0) + 1 == label)
    rank_hot = one_hot(iota((cap, rows_here), 0) == rank, F32)
    loads[2].wait()
    emb = emb_ref[...]
    per_step = max(1, 256 // cap)
    for g0 in range(0, groups, per_step):
        placed = jnp.concatenate(
            [(rank_hot * owner_hot[g : g + 1]).astype(BF16) for g in range(g0, min(g0 + per_step, groups))], axis=0
        )
        outgoing[g0 : g0 + per_step] = dot(placed, emb).astype(BF16).reshape(per_step, cap, width)

    def row_copy(to, landed):
        return pltpu.make_async_remote_copy(
            src_ref=outgoing.at[to], dst_ref=keys.at[part, me],
            send_sem=row_send.at[0], recv_sem=row_recv.at[landed],
            device_id=device(to, part), device_id_type=MESH,
        )

    def id_copy(to):
        return pltpu.make_async_remote_copy(
            src_ref=out_ids.at[to], dst_ref=key_ids.at[part, me],
            send_sem=id_send.at[0], recv_sem=id_recv.at[0],
            device_id=device(to, part), device_id_type=MESH,
        )

    def forward(src, chosen, d, home, landed):
        return pltpu.make_async_remote_copy(
            src_ref=src, dst_ref=keys.at[home, chosen],
            send_sem=fwd_send.at[d - 1], recv_sem=fwd_recv.at[d - 1, landed],
            device_id=device(me, sibling(d)), device_id_type=MESH,
        )

    def forward_ids(d, home):
        return pltpu.make_async_remote_copy(
            src_ref=key_ids.at[home], dst_ref=key_ids.at[home],
            send_sem=idf_send.at[d - 1], recv_sem=idf_recv.at[d - 1],
            device_id=device(me, sibling(d)), device_id_type=MESH,
        )

    def received(sem, ref):
        pltpu.make_async_copy(ref, ref, sem).wait()

    def send(step, ids=True, rows=True, chosen=slice(None)):
        if ids:
            for q in peers(step):
                id_copy(q).start()
        if rows:
            far = step in (outward, inward)
            landed = jnp.where(inner, classes + place, level) if far else level
            for q in peers(step)[chosen]:
                row_copy(q, landed).start()

    pl.semaphore_wait(barrier, groups - 1 + parts - 1 - jnp.where(late, 0, per_class))

    @pl.when(late)
    def _():
        for q in beyond:
            tell(ready, q)

    outward, inward, nearby, same = farthest_first

    @pl.when(level < classes // 2)
    def _():
        send(inward, rows=False)
        send(same, rows=False)
        send(nearby, rows=False)
        @pl.when(level == 0)
        def _():
            send(inward, ids=False, chosen=slice(0, 4))
            send(same, ids=False)
            pl.semaphore_wait(ready, per_class)
            send(outward)
            send(nearby, ids=False)

        @pl.when(level != 0)
        def _():
            send(inward, ids=False, chosen=slice(0, 2))
            send(same, ids=False)
            send(nearby, ids=False, chosen=slice(0, 2))
            pl.semaphore_wait(ready, per_class)
            send(outward)
            send(nearby, ids=False, chosen=slice(2, None))
            send(inward, ids=False, chosen=slice(2, None))


    @pl.when(level >= classes // 2)
    def _():
        for step in (outward, inward, same, nearby):
            if step == nearby:
                @pl.when(jnp.logical_not(late))
                def _():
                    pl.semaphore_wait(ready, per_class)
            if step == outward:
                send(inward, rows=False)
                send(same, rows=False)
            send(step, ids=step in (outward, nearby))

    for d in range(1, parts):
        forward(outgoing.at[me], me, d, part, level).start()
    keys[part, me] = outgoing[me]
    key_ids[part, me] = out_ids[me]

    def take(step):
        c = class_at(step)
        if step == (0, 0):
            received(row_recv.at[c], keys.at[part, pl.ds(0, per_class - 1)])
            for q in peers(step):
                for d in range(1, parts):
                    forward(keys.at[part, q], q, d, part, c).start()
        else:
            chosen = class_rows(c)
            received(row_recv.at[c], keys.at[part, chosen])
            for d in range(1, parts):
                forward(keys.at[part, chosen], chosen, d, part, c).start()

    def take_last():
        c = class_at(last)
        for i, q in enumerate(peers(last)):
            row_copy(q, classes + q % per_class).wait_recv()
            for d in range(1, parts):
                forward(keys.at[part, q], q, d, part, c).start()

    def class_rows(c):
        return pl.ds(c * per_class, per_class)

    def home_of(d):
        return (part + parts - d) % parts

    def take_forwarded(d, step):
        c = class_at(step)
        received(fwd_recv.at[d - 1, c], keys.at[home_of(d), class_rows(c)])

    def read_ids(piece):
        for c in range(classes):
            row = key_ids[piece, c * per_class]
            for j in range(1, per_class):
                row = row + key_ids[piece, c * per_class + j]
            id_cols[piece, c] = jnp.transpose(jnp.broadcast_to(row, (LANES, LANES)))
            yield row

    take(arriving[0])
    received(id_recv.at[0], key_ids.at[part, pl.ds(0, groups - 1)])
    for d in range(1, parts):
        forward_ids(d, part).start()
    for c, row in enumerate(read_ids(part)):
        id_rows[c] = row
    take(arriving[1])
    for d in range(1, parts):
        home = home_of(d)
        received(idf_recv.at[d - 1], key_ids.at[home])
        for _ in read_ids(home):
            pass
    for step in arriving[2:-1]:
        take(step)

    scale = 1.0 / math.sqrt(width)
    to_base_2 = scale / math.log(2.0)
    eye = iota((LANES, LANES), 0) == iota((LANES, LANES), 1)

    def block(piece, step):
        return keys[piece, class_rows(class_at(step))].reshape(LANES, width)

    def tiled(hit, raw):
        return jnp.where(hit, raw, FLOOR_SCORE).reshape(raw.shape[0] // SUBLANES, SUBLANES, LANES)

    def masked(raw, piece, key_step, query_step, own):
        hit = id_cols[piece, class_at(key_step)] == id_rows[class_at(query_step)]
        if own and key_step == query_step:
            hit = hit & jnp.logical_not(eye)
        return tiled(hit, raw)

    def weigh(x):
        return jnp.exp2(x * to_base_2)

    def summed(tiles):
        high = functools.reduce(jnp.maximum, [jnp.max(t, axis=0) for t in tiles])
        total = functools.reduce(jnp.add, [jnp.sum(weigh(t - high[None]), axis=0) for t in tiles])
        return high, total

    def merged(a, b):
        high = jnp.maximum(a[0], b[0])
        return high, a[1] * weigh(a[0] - high) + b[1] * weigh(b[0] - high)

    def scored(piece, key_step, queries, query_steps, own):
        raw = dot_transposed(block(piece, key_step), queries)
        return [
            masked(raw[:, i * LANES : (i + 1) * LANES], piece, key_step, step, own)
            for i, step in enumerate(query_steps)
        ]

    for d in range(1, parts):
        for step in old:
            take_forwarded(d, step)
    old_queries = jnp.concatenate([block(part, step) for step in old], axis=0)
    stats = None
    for d in range(parts):
        for key_step in old:
            tiles = scored(sibling(d), key_step, old_queries, old, d == 0)
            fresh = [summed([t]) for t in tiles]
            stats = fresh if stats is None else [merged(a, b) for a, b in zip(stats, fresh)]

    diagonal = iota((local_clusters, LANES), 0) == iota((local_clusters, LANES), 1)
    cluster_label = (iota((local_clusters, LANES), 0) + 1).astype(F32)

    def spread(column):
        return jnp.sum(jnp.where(diagonal, column, 0.0), axis=0, keepdims=True)

    members = jnp.zeros((local_clusters, LANES), F32)
    for c in range(classes):
        members = members + jnp.where(id_rows[c] == cluster_label, 1.0, 0.0)
    count_row = spread(jnp.sum(members, axis=1, keepdims=True))

    take_last()
    all_steps = old + [last]
    queries = jnp.concatenate([block(part, step) for step in all_steps], axis=0)
    last_queries = block(part, last)
    fresh = [summed([t]) for t in scored(part, last, queries, all_steps, True)]
    for d in range(parts):
        for key_step in old:
            fresh[-1] = merged(
                fresh[-1], summed(scored(sibling(d), key_step, last_queries, [last], d == 0))
            )
    stats = [merged(a, b) for a, b in zip(stats, fresh)] + [fresh[-1]]
    for d in range(1, parts):
        take_forwarded(d, last)
        fresh = [summed([t]) for t in scored(home_of(d), last, queries, all_steps, False)]
        stats = [merged(a, b) for a, b in zip(stats, fresh)]

    cluster_sum = jnp.zeros((local_clusters, LANES), F32)
    kept = []
    for step, (high, total) in zip(all_steps, stats):
        highest = jnp.max(high, axis=0, keepdims=True)
        total = jnp.sum(total * weigh(high - highest), axis=0, keepdims=True)
        density = highest * scale + jnp.log(total)
        id_row = id_rows[class_at(step)]
        kept.append(jnp.where(id_row > 0.5, density, 0.0))
        cluster_sum = cluster_sum + jnp.where(id_row == cluster_label, density, 0.0)
    sum_row = spread(jnp.sum(cluster_sum, axis=1, keepdims=True))
    for step, row in zip(all_steps, kept):
        result[class_at(step)] = jnp.concatenate([row, sum_row, count_row, count_row], axis=0)

    def ret_copy(to, d):
        return pltpu.make_async_remote_copy(
            src_ref=result.at[to // per_class], dst_ref=returned.at[part * groups + me],
            send_sem=ret_send.at[0], recv_sem=ret_recv.at[0],
            device_id=device(to, sibling(d)), device_id_type=MESH,
        )

    first, second = farthest_first[0], farthest_first[2]
    def give(step):
        for q in peers(step):
            for d in range(parts):
                ret_copy(q, d).start()

    @pl.when(level == 1)
    def _():
        for step in (nearby, outward, inward, same):
            give(step)

    @pl.when(level != 1)
    def _():
        for step in farthest_first:
            give(step)

    for d in range(1, parts):
        ret_copy(me, d).start()
    returned[part * groups + me] = result[level]

    received(row_send.at[0], outgoing.at[pl.ds(0, groups - 1)])
    received(id_send.at[0], out_ids.at[pl.ds(0, groups - 1)])
    for d in range(1, parts):
        received(fwd_send.at[d - 1], outgoing)
        received(idf_send.at[d - 1], out_ids)

    received(ret_recv.at[0], returned.at[pl.ds(0, parts * groups - 1)])
    back = jnp.concatenate([returned[part * groups + g, 0:1] for g in range(groups)], axis=0)
    totals = [
        functools.reduce(jnp.add, [
            jnp.concatenate([returned[piece * groups + g, at : at + 1] for g in range(groups)], axis=0)
            for piece in range(parts)
        ])
        for at in (1, 2)
    ]
    mean = totals[0] / jnp.maximum(totals[1], 1.0)
    left = jnp.concatenate([back, -mean], axis=1)
    pieces = []
    for _ in range(3):
        rounded = left.astype(BF16)
        pieces.append(rounded)
        left = left - rounded.astype(F32)
    picked = dot(jnp.concatenate(pieces, axis=0), jnp.concatenate([lane_hit, local_hit], axis=0))
    picked = picked[:groups] + (picked[groups : 2 * groups] + picked[2 * groups :])
    out_ref[...] = jnp.sum(owner_hot * picked, axis=0)
    received(ret_send.at[0], returned.at[pl.ds(0, parts * groups - 1)])


def on_device(embeddings, cluster_id, owner_map):
    rows_here, width = embeddings.shape
    clusters_all = owner_map.shape[0]
    groups = lax.axis_size("rows")
    parts = lax.axis_size("split")
    cap = 2 * rows_here // groups
    classes = groups * cap // LANES
    local_clusters = clusters_all // groups
    dma = pltpu.SemaphoreType.DMA
    return pl.pallas_call(
        functools.partial(kernel, groups, parts, local_clusters),
        out_shape=pltpu.VMEM((rows_here,), F32),
        in_specs=[pl.BlockSpec(memory_space=pl.ANY)] * 3,
        out_specs=pl.BlockSpec(memory_space=pltpu.VMEM),
        scratch_shapes=[
            pltpu.VMEM((rows_here, width), BF16),
            pltpu.VMEM((1, rows_here), jnp.int32),
            pltpu.VMEM((1, clusters_all), jnp.int32),
            pltpu.VMEM((groups, cap, width), BF16),
            pltpu.VMEM((groups, 1, LANES), F32),
            pltpu.VMEM((parts, groups, cap, width), BF16),
            pltpu.VMEM((parts, groups, 1, LANES), F32),
            pltpu.VMEM((classes, 1, LANES), F32),
            pltpu.VMEM((parts, classes, LANES, LANES), F32),
            pltpu.VMEM((classes, 4, LANES), F32),
            pltpu.VMEM((parts * groups, 4, LANES), F32),
            dma((3,)), dma((1,)), dma((classes + LANES // cap,)), dma((1,)), dma((1,)),
            dma((parts - 1,)), dma((parts - 1, classes)), dma((parts - 1,)), dma((parts - 1,)), dma((1,)), dma((1,)),
            pltpu.SemaphoreType.REGULAR,
        ],
        compiler_params=pltpu.CompilerParams(
            collective_id=0, has_side_effects=True, vmem_limit_bytes=60 * 1024 * 1024
        ),
        name="soft_neighbour",
    )(embeddings, cluster_id.reshape(1, rows_here), owner_map.reshape(1, clusters_all))


def solution(mesh):
    placed = (P(("rows", "split"), None), P(("rows", "split")), P())
    return jax.shard_map(
        on_device, mesh=mesh, in_specs=placed, out_specs=P(("rows", "split")), check_vma=False
    )
```

```python
import functools
import math

import jax
import jax.numpy as jnp
from jax import lax
from jax.experimental import pallas as pl
from jax.experimental.pallas import tpu as pltpu
from jax.sharding import PartitionSpec as P

FLOOR_SCORE = -1e30
LANES = 128
SUBLANES = 8
MESH = pl.DeviceIdType.MESH
F32 = jnp.float32
BF16 = jnp.bfloat16


def iota(shape, dim):
    return lax.broadcasted_iota(jnp.int32, shape, dim)


def one_hot(hit, dtype=BF16):
    return jnp.where(hit, 1.0, 0.0).astype(dtype)


def dot(a, b, dims=((1,), (0,))):
    return lax.dot_general(a, b, (dims, ((), ())), preferred_element_type=F32)


def dot_transposed(a, b):
    return dot(a, b, ((1,), (1,)))


def kernel(
    groups, parts, local_clusters,
    emb_in, cid_in, owner_in, out_ref,
    emb_ref, cid_ref, owner_ref,
    outgoing, out_ids, keys, key_ids, id_rows, id_cols, result, returned,
    load_sem, row_send, row_recv, id_send, id_recv,
    fwd_send, fwd_recv, idf_send, idf_recv, ret_send, ret_recv, ready,
):
    rows_here, width = emb_ref.shape
    clusters_all = owner_ref.shape[1]
    cap = outgoing.shape[1]
    per_class = LANES // cap
    classes = groups // per_class
    r, s = lax.axis_index("rows"), lax.axis_index("split")
    me = (r // parts) * parts + s
    part = r % parts
    level, place = me // per_class, me % per_class
    half = per_class // 2
    inner = (level > 0) & (level < classes - 1)

    def device(group, piece):
        return ((group // parts) * parts + piece, group % parts)

    def sibling(d):
        return (part + d) % parts

    def class_at(step):
        outer_step, inner_step = step
        if outer_step == inner_step:
            return jnp.bitwise_xor(level, outer_step)
        return jnp.bitwise_xor(level, jnp.where(inner, inner_step, outer_step))

    def peers(step):
        near = step == (0, 0)
        start = class_at(step) * per_class
        return [start + jnp.bitwise_xor(place, j) for j in reversed(range(1 if near else 0, per_class))]

    if classes == 4:
        farthest_first = [(3, 2), (2, 3), (1, 1), (0, 0)]
        arriving = [(0, 0), (3, 2), (1, 1), (2, 3)]
    else:
        farthest_first = [(k, k) for k in reversed(range(classes))]
        arriving = [(k, k) for k in range(classes)]
    last, old = arriving[-1], arriving[:-1]
    others = [q for step in farthest_first for q in peers(step)]

    loads = [
        pltpu.make_async_copy(given, held, load_sem.at[i])
        for i, (given, held) in enumerate(((cid_in, cid_ref), (owner_in, owner_ref), (emb_in, emb_ref)))
    ]
    for load in loads:
        load.start()

    barrier = pltpu.get_barrier_semaphore()

    def tell(semaphore, q):
        pl.semaphore_signal(semaphore, inc=1, device_id=device(q, part), device_id_type=MESH)

    beside = peers((0, 0))
    beyond = [q for step in farthest_first[:-1] for q in peers(step)]
    late = level == classes - 1

    @pl.when(jnp.logical_not(late))
    def _():
        for q in beyond:
            tell(barrier, q)

    for q in beside:
        tell(barrier, q)
    for d in range(1, parts):
        pl.semaphore_signal(barrier, inc=1, device_id=device(me, sibling(d)), device_id_type=MESH)

    before = one_hot(iota((rows_here, rows_here), 0) < iota((rows_here, rows_here), 1))
    before_cl = one_hot(iota((clusters_all, clusters_all), 0) < iota((clusters_all, clusters_all), 1))
    loads[0].wait()
    loads[1].wait()
    cid = cid_ref[...]
    cluster_hit = one_hot(iota((clusters_all, rows_here), 0) == cid)
    owner_cl = iota((groups, clusters_all), 0) == owner_ref[...]
    local_rank = dot(one_hot(owner_cl), before_cl)
    label_cl = jnp.where(owner_cl, local_rank + 1.0, 0.0).astype(BF16)
    labels = dot(label_cl, cluster_hit)
    owner_hot = jnp.where(labels > 0.5, 1.0, 0.0)
    prefix = dot(owner_hot.astype(BF16), before)
    rank = jnp.sum(owner_hot * prefix, axis=0, keepdims=True).astype(jnp.int32)
    lane_hit = one_hot(iota((LANES, rows_here), 0) == rank + place * cap)
    id_block = dot_transposed(labels.astype(BF16), lane_hit)
    for g in range(groups):
        out_ids[g] = id_block[g : g + 1]
    label = jnp.sum(labels, axis=0, keepdims=True).astype(jnp.int32)
    local_hit = one_hot(iota((LANES, rows_here), 0) + 1 == label)
    rank_hot = one_hot(iota((cap, rows_here), 0) == rank, F32)
    loads[2].wait()
    emb = emb_ref[...]
    per_step = max(1, 256 // cap)
    for g0 in range(0, groups, per_step):
        placed = jnp.concatenate(
            [(rank_hot * owner_hot[g : g + 1]).astype(BF16) for g in range(g0, min(g0 + per_step, groups))], axis=0
        )
        outgoing[g0 : g0 + per_step] = dot(placed, emb).astype(BF16).reshape(per_step, cap, width)

    def row_copy(to, landed):
        return pltpu.make_async_remote_copy(
            src_ref=outgoing.at[to], dst_ref=keys.at[part, me],
            send_sem=row_send.at[0], recv_sem=row_recv.at[landed],
            device_id=device(to, part), device_id_type=MESH,
        )

    def id_copy(to):
        return pltpu.make_async_remote_copy(
            src_ref=out_ids.at[to], dst_ref=key_ids.at[part, me],
            send_sem=id_send.at[0], recv_sem=id_recv.at[0],
            device_id=device(to, part), device_id_type=MESH,
        )

    def forward(src, chosen, d, home, landed):
        return pltpu.make_async_remote_copy(
            src_ref=src, dst_ref=keys.at[home, chosen],
            send_sem=fwd_send.at[d - 1], recv_sem=fwd_recv.at[d - 1, landed],
            device_id=device(me, sibling(d)), device_id_type=MESH,
        )

    def forward_ids(d, home):
        return pltpu.make_async_remote_copy(
            src_ref=key_ids.at[home], dst_ref=key_ids.at[home],
            send_sem=idf_send.at[d - 1], recv_sem=idf_recv.at[d - 1],
            device_id=device(me, sibling(d)), device_id_type=MESH,
        )

    def received(sem, ref):
        pltpu.make_async_copy(ref, ref, sem).wait()

    def send(step, ids=True, rows=True, chosen=slice(None)):
        if ids:
            for q in peers(step):
                id_copy(q).start()
        if rows:
            far = step in (outward, inward)
            landed = jnp.where(inner, classes + place, level) if far else level
            for q in peers(step)[chosen]:
                row_copy(q, landed).start()

    pl.semaphore_wait(barrier, groups - 1 + parts - 1 - jnp.where(late, 0, per_class))

    @pl.when(late)
    def _():
        for q in beyond:
            tell(ready, q)

    outward, inward, nearby, same = farthest_first

    @pl.when(level < classes // 2)
    def _():
        send(inward, rows=False)
        send(same, rows=False)
        send(nearby, rows=False)

        def send_early(first):
            send(inward, ids=False, chosen=slice(0, first))
            send(same, ids=False)
            send(nearby, ids=False, chosen=slice(0, half))
            pl.semaphore_wait(ready, per_class)
            send(outward)

        @pl.when(level == 0)
        def _():
            send_early(per_class - 1)
            send(inward, ids=False, chosen=slice(per_class - 1, None))
            send(nearby, ids=False, chosen=slice(half, None))

        @pl.when(level != 0)
        def _():
            send_early(half)
            send(nearby, ids=False, chosen=slice(half, None))
            send(inward, ids=False, chosen=slice(half, None))

    @pl.when(level >= classes // 2)
    def _():
        for step in (outward, inward, same, nearby):
            if step == nearby:
                @pl.when(jnp.logical_not(late))
                def _():
                    pl.semaphore_wait(ready, per_class)
            if step == outward:
                send(inward, rows=False)
                send(same, rows=False)
            send(step, ids=step in (outward, nearby))

    for d in range(1, parts):
        forward(outgoing.at[me], me, d, part, level).start()
    keys[part, me] = outgoing[me]
    key_ids[part, me] = out_ids[me]

    def take(step):
        c = class_at(step)
        if step == (0, 0):
            received(row_recv.at[c], keys.at[part, pl.ds(0, per_class - 1)])
            for q in peers(step):
                for d in range(1, parts):
                    forward(keys.at[part, q], q, d, part, c).start()
        else:
            chosen = class_rows(c)
            received(row_recv.at[c], keys.at[part, chosen])
            for d in range(1, parts):
                forward(keys.at[part, chosen], chosen, d, part, c).start()

    def take_last():
        c = class_at(last)
        for i, q in enumerate(peers(last)):
            row_copy(q, classes + q % per_class).wait_recv()
            for d in range(1, parts):
                forward(keys.at[part, q], q, d, part, c).start()

    def class_rows(c):
        return pl.ds(c * per_class, per_class)

    def home_of(d):
        return (part + parts - d) % parts

    def take_forwarded(d, step):
        c = class_at(step)
        received(fwd_recv.at[d - 1, c], keys.at[home_of(d), class_rows(c)])

    def read_ids(piece):
        for c in range(classes):
            row = key_ids[piece, c * per_class]
            for j in range(1, per_class):
                row = row + key_ids[piece, c * per_class + j]
            id_cols[piece, c] = jnp.transpose(jnp.broadcast_to(row, (LANES, LANES)))
            yield row

    take(arriving[0])
    received(id_recv.at[0], key_ids.at[part, pl.ds(0, groups - 1)])
    for d in range(1, parts):
        forward_ids(d, part).start()
    for c, row in enumerate(read_ids(part)):
        id_rows[c] = row
    take(arriving[1])
    for d in range(1, parts):
        home = home_of(d)
        received(idf_recv.at[d - 1], key_ids.at[home])
        for _ in read_ids(home):
            pass
    for step in arriving[2:-1]:
        take(step)

    scale = 1.0 / math.sqrt(width)
    to_base_2 = scale / math.log(2.0)
    eye = iota((LANES, LANES), 0) == iota((LANES, LANES), 1)

    def block(piece, step):
        return keys[piece, class_rows(class_at(step))].reshape(LANES, width)

    def tiled(hit, raw):
        return jnp.where(hit, raw, FLOOR_SCORE).reshape(raw.shape[0] // SUBLANES, SUBLANES, LANES)

    def masked(raw, piece, key_step, query_step, own):
        hit = id_cols[piece, class_at(key_step)] == id_rows[class_at(query_step)]
        if own and key_step == query_step:
            hit = hit & jnp.logical_not(eye)
        return tiled(hit, raw)

    def weigh(x):
        return jnp.exp2(x * to_base_2)

    def summed(tiles):
        high = functools.reduce(jnp.maximum, [jnp.max(t, axis=0) for t in tiles])
        total = functools.reduce(jnp.add, [jnp.sum(weigh(t - high[None]), axis=0) for t in tiles])
        return high, total

    def merged(a, b):
        high = jnp.maximum(a[0], b[0])
        return high, a[1] * weigh(a[0] - high) + b[1] * weigh(b[0] - high)

    def scored(piece, key_step, queries, query_steps, own):
        raw = dot_transposed(block(piece, key_step), queries)
        return [
            masked(raw[:, i * LANES : (i + 1) * LANES], piece, key_step, step, own)
            for i, step in enumerate(query_steps)
        ]

    for d in range(1, parts):
        for step in old:
            take_forwarded(d, step)
    old_queries = jnp.concatenate([block(part, step) for step in old], axis=0)
    stats = None
    for d in range(parts):
        for key_step in old:
            tiles = scored(sibling(d), key_step, old_queries, old, d == 0)
            fresh = [summed([t]) for t in tiles]
            stats = fresh if stats is None else [merged(a, b) for a, b in zip(stats, fresh)]

    diagonal = iota((local_clusters, LANES), 0) == iota((local_clusters, LANES), 1)
    cluster_label = (iota((local_clusters, LANES), 0) + 1).astype(F32)

    def spread(column):
        return jnp.sum(jnp.where(diagonal, column, 0.0), axis=0, keepdims=True)

    members = jnp.zeros((local_clusters, LANES), F32)
    for c in range(classes):
        members = members + jnp.where(id_rows[c] == cluster_label, 1.0, 0.0)
    count_row = spread(jnp.sum(members, axis=1, keepdims=True))

    take_last()
    all_steps = old + [last]
    queries = jnp.concatenate([block(part, step) for step in all_steps], axis=0)
    last_queries = block(part, last)
    fresh = [summed([t]) for t in scored(part, last, queries, all_steps, True)]
    for d in range(parts):
        for key_step in old:
            fresh[-1] = merged(
                fresh[-1], summed(scored(sibling(d), key_step, last_queries, [last], d == 0))
            )
    stats = [merged(a, b) for a, b in zip(stats, fresh)] + [fresh[-1]]
    for d in range(1, parts):
        take_forwarded(d, last)
        fresh = [summed([t]) for t in scored(home_of(d), last, queries, all_steps, False)]
        stats = [merged(a, b) for a, b in zip(stats, fresh)]

    cluster_sum = jnp.zeros((local_clusters, LANES), F32)
    kept = []
    for step, (high, total) in zip(all_steps, stats):
        highest = jnp.max(high, axis=0, keepdims=True)
        total = jnp.sum(total * weigh(high - highest), axis=0, keepdims=True)
        density = highest * scale + jnp.log(total)
        id_row = id_rows[class_at(step)]
        kept.append(jnp.where(id_row > 0.5, density, 0.0))
        cluster_sum = cluster_sum + jnp.where(id_row == cluster_label, density, 0.0)
    sum_row = spread(jnp.sum(cluster_sum, axis=1, keepdims=True))
    for step, row in zip(all_steps, kept):
        result[class_at(step)] = jnp.concatenate([row, sum_row, count_row, count_row], axis=0)

    def ret_copy(to, d):
        return pltpu.make_async_remote_copy(
            src_ref=result.at[to // per_class], dst_ref=returned.at[part * groups + me],
            send_sem=ret_send.at[0], recv_sem=ret_recv.at[0],
            device_id=device(to, sibling(d)), device_id_type=MESH,
        )

    def give(step):
        for q in peers(step):
            for d in range(parts):
                ret_copy(q, d).start()

    @pl.when(level == 1)
    def _():
        for step in (nearby, outward, inward, same):
            give(step)

    @pl.when(level != 1)
    def _():
        for step in farthest_first:
            give(step)

    for d in range(1, parts):
        ret_copy(me, d).start()
    returned[part * groups + me] = result[level]

    received(row_send.at[0], outgoing.at[pl.ds(0, groups - 1)])
    received(id_send.at[0], out_ids.at[pl.ds(0, groups - 1)])
    for d in range(1, parts):
        received(fwd_send.at[d - 1], outgoing)
        received(idf_send.at[d - 1], out_ids)

    received(ret_recv.at[0], returned.at[pl.ds(0, parts * groups - 1)])
    back = jnp.concatenate([returned[part * groups + g, 0:1] for g in range(groups)], axis=0)
    totals = [
        functools.reduce(jnp.add, [
            jnp.concatenate([returned[piece * groups + g, at : at + 1] for g in range(groups)], axis=0)
            for piece in range(parts)
        ])
        for at in (1, 2)
    ]
    mean = totals[0] / jnp.maximum(totals[1], 1.0)
    left = jnp.concatenate([back, -mean], axis=1)
    pieces = []
    for _ in range(3):
        rounded = left.astype(BF16)
        pieces.append(rounded)
        left = left - rounded.astype(F32)
    picked = dot(jnp.concatenate(pieces, axis=0), jnp.concatenate([lane_hit, local_hit], axis=0))
    picked = picked[:groups] + (picked[groups : 2 * groups] + picked[2 * groups :])
    out_ref[...] = jnp.sum(owner_hot * picked, axis=0)
    received(ret_send.at[0], returned.at[pl.ds(0, parts * groups - 1)])


def on_device(embeddings, cluster_id, owner_map):
    rows_here, width = embeddings.shape
    clusters_all = owner_map.shape[0]
    groups = lax.axis_size("rows")
    parts = lax.axis_size("split")
    cap = 2 * rows_here // groups
    classes = groups * cap // LANES
    local_clusters = clusters_all // groups
    dma = pltpu.SemaphoreType.DMA
    return pl.pallas_call(
        functools.partial(kernel, groups, parts, local_clusters),
        out_shape=pltpu.VMEM((rows_here,), F32),
        in_specs=[pl.BlockSpec(memory_space=pl.ANY)] * 3,
        out_specs=pl.BlockSpec(memory_space=pltpu.VMEM),
        scratch_shapes=[
            pltpu.VMEM((rows_here, width), BF16),
            pltpu.VMEM((1, rows_here), jnp.int32),
            pltpu.VMEM((1, clusters_all), jnp.int32),
            pltpu.VMEM((groups, cap, width), BF16),
            pltpu.VMEM((groups, 1, LANES), F32),
            pltpu.VMEM((parts, groups, cap, width), BF16),
            pltpu.VMEM((parts, groups, 1, LANES), F32),
            pltpu.VMEM((classes, 1, LANES), F32),
            pltpu.VMEM((parts, classes, LANES, LANES), F32),
            pltpu.VMEM((classes, 4, LANES), F32),
            pltpu.VMEM((parts * groups, 4, LANES), F32),
            dma((3,)), dma((1,)), dma((classes + LANES // cap,)), dma((1,)), dma((1,)),
            dma((parts - 1,)), dma((parts - 1, classes)), dma((parts - 1,)), dma((parts - 1,)), dma((1,)), dma((1,)),
            pltpu.SemaphoreType.REGULAR,
        ],
        compiler_params=pltpu.CompilerParams(
            collective_id=0, has_side_effects=True, vmem_limit_bytes=60 * 1024 * 1024
        ),
        name="soft_neighbour",
    )(embeddings, cluster_id.reshape(1, rows_here), owner_map.reshape(1, clusters_all))


def solution(mesh):
    placed = (P(("rows", "split"), None), P(("rows", "split")), P())
    return jax.shard_map(
        on_device, mesh=mesh, in_specs=placed, out_specs=P(("rows", "split")), check_vma=False
    )
```

```python
import functools
import math

import jax
import jax.numpy as jnp
from jax import lax
from jax.experimental import pallas as pl
from jax.experimental.pallas import tpu as pltpu
from jax.sharding import PartitionSpec as P

FLOOR_SCORE = -1e30
LANES = 128
SUBLANES = 8
MESH = pl.DeviceIdType.MESH
F32 = jnp.float32
BF16 = jnp.bfloat16


def iota(shape, dim):
    return lax.broadcasted_iota(jnp.int32, shape, dim)


def one_hot(hit, dtype=BF16):
    return jnp.where(hit, 1.0, 0.0).astype(dtype)


def dot(a, b, dims=((1,), (0,))):
    return lax.dot_general(a, b, (dims, ((), ())), preferred_element_type=F32)


def dot_transposed(a, b):
    return dot(a, b, ((1,), (1,)))


def kernel(
    groups, parts, local_clusters,
    emb_in, cid_in, owner_in, out_ref,
    emb_ref, cid_ref, owner_ref,
    outgoing, out_ids, keys, key_ids, id_rows, id_cols, result, returned,
    load_sem, row_send, row_recv, id_send, id_recv,
    fwd_send, fwd_recv, idf_send, idf_recv, ret_send, ret_recv, ready,
):
    rows_here, width = emb_ref.shape
    clusters_all = owner_ref.shape[1]
    cap = outgoing.shape[1]
    per_class = LANES // cap
    classes = groups // per_class
    r, s = lax.axis_index("rows"), lax.axis_index("split")
    me = (r // parts) * parts + s
    part = r % parts
    level, place = me // per_class, me % per_class
    half = per_class // 2
    inner = (level > 0) & (level < classes - 1)

    def device(group, piece):
        return ((group // parts) * parts + piece, group % parts)

    def sibling(d):
        return (part + d) % parts

    def class_at(step):
        outer_step, inner_step = step
        if outer_step == inner_step:
            return jnp.bitwise_xor(level, outer_step)
        return jnp.bitwise_xor(level, jnp.where(inner, inner_step, outer_step))

    def peers(step):
        near = step == (0, 0)
        start = class_at(step) * per_class
        return [start + jnp.bitwise_xor(place, j) for j in reversed(range(1 if near else 0, per_class))]

    if classes == 4:
        farthest_first = [(3, 2), (2, 3), (1, 1), (0, 0)]
        arriving = [(0, 0), (3, 2), (1, 1), (2, 3)]
    else:
        farthest_first = [(k, k) for k in reversed(range(classes))]
        arriving = [(k, k) for k in range(classes)]
    last, old = arriving[-1], arriving[:-1]
    others = [q for step in farthest_first for q in peers(step)]

    loads = [
        pltpu.make_async_copy(given, held, load_sem.at[i])
        for i, (given, held) in enumerate(((cid_in, cid_ref), (owner_in, owner_ref), (emb_in, emb_ref)))
    ]
    for load in loads:
        load.start()

    barrier = pltpu.get_barrier_semaphore()

    def tell(semaphore, q):
        pl.semaphore_signal(semaphore, inc=1, device_id=device(q, part), device_id_type=MESH)

    beside = peers((0, 0))
    beyond = [q for step in farthest_first[:-1] for q in peers(step)]
    late = level == classes - 1

    @pl.when(jnp.logical_not(late))
    def _():
        for q in beyond:
            tell(barrier, q)

    for q in beside:
        tell(barrier, q)
    for d in range(1, parts):
        pl.semaphore_signal(barrier, inc=1, device_id=device(me, sibling(d)), device_id_type=MESH)

    before = one_hot(iota((rows_here, rows_here), 0) < iota((rows_here, rows_here), 1))
    before_cl = one_hot(iota((clusters_all, clusters_all), 0) < iota((clusters_all, clusters_all), 1))
    loads[0].wait()
    loads[1].wait()
    cid = cid_ref[...]
    cluster_hit = one_hot(iota((clusters_all, rows_here), 0) == cid)
    owner_cl = iota((groups, clusters_all), 0) == owner_ref[...]
    local_rank = dot(one_hot(owner_cl), before_cl)
    label_cl = jnp.where(owner_cl, local_rank + 1.0, 0.0).astype(BF16)
    labels = dot(label_cl, cluster_hit)
    owner_hot = jnp.where(labels > 0.5, 1.0, 0.0)
    prefix = dot(owner_hot.astype(BF16), before)
    rank = jnp.sum(owner_hot * prefix, axis=0, keepdims=True).astype(jnp.int32)
    lane_hit = one_hot(iota((LANES, rows_here), 0) == rank + place * cap)
    id_block = dot_transposed(labels.astype(BF16), lane_hit)
    for g in range(groups):
        out_ids[g] = id_block[g : g + 1]
    label = jnp.sum(labels, axis=0, keepdims=True).astype(jnp.int32)
    local_hit = one_hot(iota((LANES, rows_here), 0) + 1 == label)
    rank_hot = one_hot(iota((cap, rows_here), 0) == rank, F32)
    loads[2].wait()
    emb = emb_ref[...]
    per_step = max(1, 256 // cap)
    for g0 in range(0, groups, per_step):
        placed = jnp.concatenate(
            [(rank_hot * owner_hot[g : g + 1]).astype(BF16) for g in range(g0, min(g0 + per_step, groups))], axis=0
        )
        outgoing[g0 : g0 + per_step] = dot(placed, emb).astype(BF16).reshape(per_step, cap, width)

    def row_copy(to, landed):
        return pltpu.make_async_remote_copy(
            src_ref=outgoing.at[to], dst_ref=keys.at[part, me],
            send_sem=row_send.at[0], recv_sem=row_recv.at[landed],
            device_id=device(to, part), device_id_type=MESH,
        )

    def id_copy(to):
        return pltpu.make_async_remote_copy(
            src_ref=out_ids.at[to], dst_ref=key_ids.at[part, me],
            send_sem=id_send.at[0], recv_sem=id_recv.at[0],
            device_id=device(to, part), device_id_type=MESH,
        )

    def forward(src, chosen, d, home, landed):
        return pltpu.make_async_remote_copy(
            src_ref=src, dst_ref=keys.at[home, chosen],
            send_sem=fwd_send.at[d - 1], recv_sem=fwd_recv.at[d - 1, landed],
            device_id=device(me, sibling(d)), device_id_type=MESH,
        )

    def forward_ids(d, home):
        return pltpu.make_async_remote_copy(
            src_ref=key_ids.at[home], dst_ref=key_ids.at[home],
            send_sem=idf_send.at[d - 1], recv_sem=idf_recv.at[d - 1],
            device_id=device(me, sibling(d)), device_id_type=MESH,
        )

    def received(sem, ref):
        pltpu.make_async_copy(ref, ref, sem).wait()

    def send(step, ids=True, rows=True, chosen=slice(None)):
        if ids:
            for q in peers(step):
                id_copy(q).start()
        if rows:
            far = step in (outward, inward)
            landed = jnp.where(inner, classes + place, level) if far else level
            for q in peers(step)[chosen]:
                row_copy(q, landed).start()

    pl.semaphore_wait(barrier, groups - 1 + parts - 1 - jnp.where(late, 0, per_class))

    @pl.when(late)
    def _():
        for q in beyond:
            tell(ready, q)

    outward, inward, nearby, same = farthest_first

    @pl.when(level < classes // 2)
    def _():
        send(inward, rows=False)
        send(same, rows=False)
        send(nearby, rows=False)

        def send_early(first):
            send(inward, ids=False, chosen=slice(0, first))
            send(same, ids=False)
            send(nearby, ids=False, chosen=slice(0, half))
            pl.semaphore_wait(ready, per_class)
            send(outward)

        @pl.when(level == 0)
        def _():
            send_early(per_class - 1)
            send(inward, ids=False, chosen=slice(per_class - 1, None))
            send(nearby, ids=False, chosen=slice(half, None))

        @pl.when(level != 0)
        def _():
            send_early(half)
            send(nearby, ids=False, chosen=slice(half, None))
            send(inward, ids=False, chosen=slice(half, None))

    @pl.when(level >= classes // 2)
    def _():
        send(outward, rows=False)
        send(inward, rows=False)
        send(same, rows=False)
        send(outward, ids=False)

        @pl.when(late)
        def _():
            send(inward, ids=False, chosen=slice(0, half))
            send(nearby, chosen=slice(0, half))
            send(same, ids=False)
            send(inward, ids=False, chosen=slice(half, None))
            send(nearby, ids=False, chosen=slice(half, None))

        @pl.when(jnp.logical_not(late))
        def _():
            send(inward, ids=False)
            send(same, ids=False)
            pl.semaphore_wait(ready, per_class)
            send(nearby)

    for d in range(1, parts):
        forward(outgoing.at[me], me, d, part, level).start()
    keys[part, me] = outgoing[me]
    key_ids[part, me] = out_ids[me]

    def take(step):
        c = class_at(step)
        if step == (0, 0):
            received(row_recv.at[c], keys.at[part, pl.ds(0, per_class - 1)])
            for q in peers(step):
                for d in range(1, parts):
                    forward(keys.at[part, q], q, d, part, c).start()
        else:
            chosen = class_rows(c)
            received(row_recv.at[c], keys.at[part, chosen])
            for d in range(1, parts):
                forward(keys.at[part, chosen], chosen, d, part, c).start()

    def take_last():
        c = class_at(last)
        for i, q in enumerate(peers(last)):
            row_copy(q, classes + q % per_class).wait_recv()
            for d in range(1, parts):
                forward(keys.at[part, q], q, d, part, c).start()

    def class_rows(c):
        return pl.ds(c * per_class, per_class)

    def home_of(d):
        return (part + parts - d) % parts

    def take_forwarded(d, step):
        c = class_at(step)
        received(fwd_recv.at[d - 1, c], keys.at[home_of(d), class_rows(c)])

    def read_ids(piece):
        for c in range(classes):
            row = key_ids[piece, c * per_class]
            for j in range(1, per_class):
                row = row + key_ids[piece, c * per_class + j]
            id_cols[piece, c] = jnp.transpose(jnp.broadcast_to(row, (LANES, LANES)))
            yield row

    take(arriving[0])
    received(id_recv.at[0], key_ids.at[part, pl.ds(0, groups - 1)])
    for d in range(1, parts):
        forward_ids(d, part).start()
    for c, row in enumerate(read_ids(part)):
        id_rows[c] = row
    take(arriving[1])
    for d in range(1, parts):
        home = home_of(d)
        received(idf_recv.at[d - 1], key_ids.at[home])
        for _ in read_ids(home):
            pass
    for step in arriving[2:-1]:
        take(step)

    scale = 1.0 / math.sqrt(width)
    to_base_2 = scale / math.log(2.0)
    eye = iota((LANES, LANES), 0) == iota((LANES, LANES), 1)

    def block(piece, step):
        return keys[piece, class_rows(class_at(step))].reshape(LANES, width)

    def tiled(hit, raw):
        return jnp.where(hit, raw, FLOOR_SCORE).reshape(raw.shape[0] // SUBLANES, SUBLANES, LANES)

    def masked(raw, piece, key_step, query_step, own):
        hit = id_cols[piece, class_at(key_step)] == id_rows[class_at(query_step)]
        if own and key_step == query_step:
            hit = hit & jnp.logical_not(eye)
        return tiled(hit, raw)

    def weigh(x):
        return jnp.exp2(x * to_base_2)

    def summed(tiles):
        high = functools.reduce(jnp.maximum, [jnp.max(t, axis=0) for t in tiles])
        total = functools.reduce(jnp.add, [jnp.sum(weigh(t - high[None]), axis=0) for t in tiles])
        return high, total

    def merged(a, b):
        high = jnp.maximum(a[0], b[0])
        return high, a[1] * weigh(a[0] - high) + b[1] * weigh(b[0] - high)

    def scored(piece, key_step, queries, query_steps, own):
        raw = dot_transposed(block(piece, key_step), queries)
        return [
            masked(raw[:, i * LANES : (i + 1) * LANES], piece, key_step, step, own)
            for i, step in enumerate(query_steps)
        ]

    for d in range(1, parts):
        for step in old:
            take_forwarded(d, step)
    old_queries = jnp.concatenate([block(part, step) for step in old], axis=0)
    stats = None
    for d in range(parts):
        for key_step in old:
            tiles = scored(sibling(d), key_step, old_queries, old, d == 0)
            fresh = [summed([t]) for t in tiles]
            stats = fresh if stats is None else [merged(a, b) for a, b in zip(stats, fresh)]

    diagonal = iota((local_clusters, LANES), 0) == iota((local_clusters, LANES), 1)
    cluster_label = (iota((local_clusters, LANES), 0) + 1).astype(F32)

    def spread(column):
        return jnp.sum(jnp.where(diagonal, column, 0.0), axis=0, keepdims=True)

    members = jnp.zeros((local_clusters, LANES), F32)
    for c in range(classes):
        members = members + jnp.where(id_rows[c] == cluster_label, 1.0, 0.0)
    count_row = spread(jnp.sum(members, axis=1, keepdims=True))

    take_last()
    all_steps = old + [last]
    queries = jnp.concatenate([block(part, step) for step in all_steps], axis=0)
    last_queries = block(part, last)
    fresh = [summed([t]) for t in scored(part, last, queries, all_steps, True)]
    for d in range(parts):
        for key_step in old:
            fresh[-1] = merged(
                fresh[-1], summed(scored(sibling(d), key_step, last_queries, [last], d == 0))
            )
    stats = [merged(a, b) for a, b in zip(stats, fresh)] + [fresh[-1]]
    for d in range(1, parts):
        take_forwarded(d, last)
        fresh = [summed([t]) for t in scored(home_of(d), last, queries, all_steps, False)]
        stats = [merged(a, b) for a, b in zip(stats, fresh)]

    cluster_sum = jnp.zeros((local_clusters, LANES), F32)
    kept = []
    for step, (high, total) in zip(all_steps, stats):
        highest = jnp.max(high, axis=0, keepdims=True)
        total = jnp.sum(total * weigh(high - highest), axis=0, keepdims=True)
        density = highest * scale + jnp.log(total)
        id_row = id_rows[class_at(step)]
        kept.append(jnp.where(id_row > 0.5, density, 0.0))
        cluster_sum = cluster_sum + jnp.where(id_row == cluster_label, density, 0.0)
    sum_row = spread(jnp.sum(cluster_sum, axis=1, keepdims=True))
    for step, row in zip(all_steps, kept):
        result[class_at(step)] = jnp.concatenate([row, sum_row, count_row, count_row], axis=0)

    def ret_copy(to, d):
        return pltpu.make_async_remote_copy(
            src_ref=result.at[to // per_class], dst_ref=returned.at[part * groups + me],
            send_sem=ret_send.at[0], recv_sem=ret_recv.at[0],
            device_id=device(to, sibling(d)), device_id_type=MESH,
        )

    def give(step):
        for q in peers(step):
            for d in range(parts):
                ret_copy(q, d).start()

    @pl.when(level == 1)
    def _():
        for step in (nearby, outward, inward, same):
            give(step)

    @pl.when(level != 1)
    def _():
        for step in farthest_first:
            give(step)

    for d in range(1, parts):
        ret_copy(me, d).start()
    returned[part * groups + me] = result[level]

    received(row_send.at[0], outgoing.at[pl.ds(0, groups - 1)])
    received(id_send.at[0], out_ids.at[pl.ds(0, groups - 1)])
    for d in range(1, parts):
        received(fwd_send.at[d - 1], outgoing)
        received(idf_send.at[d - 1], out_ids)

    received(ret_recv.at[0], returned.at[pl.ds(0, parts * groups - 1)])
    back = jnp.concatenate([returned[part * groups + g, 0:1] for g in range(groups)], axis=0)
    totals = [
        functools.reduce(jnp.add, [
            jnp.concatenate([returned[piece * groups + g, at : at + 1] for g in range(groups)], axis=0)
            for piece in range(parts)
        ])
        for at in (1, 2)
    ]
    mean = totals[0] / jnp.maximum(totals[1], 1.0)
    left = jnp.concatenate([back, -mean], axis=1)
    pieces = []
    for _ in range(3):
        rounded = left.astype(BF16)
        pieces.append(rounded)
        left = left - rounded.astype(F32)
    picked = dot(jnp.concatenate(pieces, axis=0), jnp.concatenate([lane_hit, local_hit], axis=0))
    picked = picked[:groups] + (picked[groups : 2 * groups] + picked[2 * groups :])
    out_ref[...] = jnp.sum(owner_hot * picked, axis=0)
    received(ret_send.at[0], returned.at[pl.ds(0, parts * groups - 1)])


def on_device(embeddings, cluster_id, owner_map):
    rows_here, width = embeddings.shape
    clusters_all = owner_map.shape[0]
    groups = lax.axis_size("rows")
    parts = lax.axis_size("split")
    cap = 2 * rows_here // groups
    classes = groups * cap // LANES
    local_clusters = clusters_all // groups
    dma = pltpu.SemaphoreType.DMA
    return pl.pallas_call(
        functools.partial(kernel, groups, parts, local_clusters),
        out_shape=pltpu.VMEM((rows_here,), F32),
        in_specs=[pl.BlockSpec(memory_space=pl.ANY)] * 3,
        out_specs=pl.BlockSpec(memory_space=pltpu.VMEM),
        scratch_shapes=[
            pltpu.VMEM((rows_here, width), BF16),
            pltpu.VMEM((1, rows_here), jnp.int32),
            pltpu.VMEM((1, clusters_all), jnp.int32),
            pltpu.VMEM((groups, cap, width), BF16),
            pltpu.VMEM((groups, 1, LANES), F32),
            pltpu.VMEM((parts, groups, cap, width), BF16),
            pltpu.VMEM((parts, groups, 1, LANES), F32),
            pltpu.VMEM((classes, 1, LANES), F32),
            pltpu.VMEM((parts, classes, LANES, LANES), F32),
            pltpu.VMEM((classes, 4, LANES), F32),
            pltpu.VMEM((parts * groups, 4, LANES), F32),
            dma((3,)), dma((1,)), dma((classes + LANES // cap,)), dma((1,)), dma((1,)),
            dma((parts - 1,)), dma((parts - 1, classes)), dma((parts - 1,)), dma((parts - 1,)), dma((1,)), dma((1,)),
            pltpu.SemaphoreType.REGULAR,
        ],
        compiler_params=pltpu.CompilerParams(
            collective_id=0, has_side_effects=True, vmem_limit_bytes=60 * 1024 * 1024
        ),
        name="soft_neighbour",
    )(embeddings, cluster_id.reshape(1, rows_here), owner_map.reshape(1, clusters_all))


def solution(mesh):
    placed = (P(("rows", "split"), None), P(("rows", "split")), P())
    return jax.shard_map(
        on_device, mesh=mesh, in_specs=placed, out_specs=P(("rows", "split")), check_vma=False
    )
```
